256 devices in a mesh: space: 16 (over z, y_lo), snap: 16 (over y_hi, x, core).
Axes of the slice: x: 4, y: 4 (y_hi: 2, y_lo: 2; y = y_hi * 2 + y_lo), z: 8, core: 2. Of those that a mesh axis runs over, the one named last changes fastest.
Arguments:
- primal: bfloat16 [2048, 196608], P('snap', 'space'), may hold values from -6 to 6
- adjoint_pencils: bfloat16 [1024, 196608], P('snap', 'space'), may hold values from -0.01953125 to 0.01953125
- weights: float32 [196608], P('space'), may hold values from 0.2 to 2
- pencil_map: int32 [1536], replicated, may hold values from 0 to 1535, as said below
Outputs:
- hankel: float32 [1024, 2048], P('space', 'snap')
The draws below stay inside these ranges and needn't reach their ends.
Inputs may be any that keep to these rules, and one draw needn't show every extreme that they name: `pencil_map`: each number appears once; each aligned block of 96 entries holds exactly 6 entries from every aligned range of 96 values.
All inputs are finite; a program needn't handle non-finite values.
Results may differ from the reference program's by a relative error of at most 0.0029.
Values may be sent and summed in bfloat16 or wider, within the bound.
A program may use at most 128 MiB of HBM per device.

```python
import math
import jax
import jax.numpy as jnp
from jax import lax

MP = 2048
MA = 1024
PEN_LEN = 128
PEN_DEV = 96
PENCILS = 1536
NPTS = 196608


def draw_pencil_map(key, part):
    tiles = PENCILS // PEN_DEV
    share = PEN_DEV // tiles

    def shuffle(subkey):
        return jax.random.permutation(subkey, PEN_DEV)
    inner = jax.vmap(shuffle)(jax.random.split(jax.random.fold_in(key, 11), tiles)).astype(jnp.int32)
    slots = inner + (jnp.arange(tiles, dtype=jnp.int32) * PEN_DEV)[:, None]
    grouped = slots.reshape(tiles, tiles, share).transpose(1, 0, 2).reshape(tiles, PEN_DEV)
    mixing = jax.vmap(shuffle)(jax.random.split(jax.random.fold_in(key, 23), tiles)).astype(jnp.int32)
    return jnp.take_along_axis(grouped, mixing, axis=1).reshape(PENCILS).astype(jnp.int32)


def with_spikes(result, rng, source, target, blocks, factor):
    def block_of(position):
        return (jnp.arange(result.shape[position]) // (result.shape[position] // blocks)).reshape((-1,) + (1,) * (result.ndim - 1 - position))

    one_side = jax.random.permutation(rng, blocks)[block_of(target)]
    other_side = (block_of(target) + blocks // 2) % blocks
    return jnp.where((block_of(source) == one_side) | (block_of(source) == other_side), factor * result, result)


def levels(key, extent, pieces, smallest, largest):
    def one(axis_at, shards_of):
        heights = jax.random.uniform(jax.random.fold_in(jax.random.fold_in(key, 6), axis_at), (shards_of,), jnp.float32, smallest / len(pieces), largest / len(pieces))
        return jnp.repeat(jnp.exp(heights), extent[axis_at] // shards_of).reshape((-1,) + (1,) * (len(extent) - axis_at - 1))

    gain = one(*pieces[0])
    for cut in pieces[1:]:
        gain = gain * one(*cut)
    return gain


def centred(key, shape, scale, reach, cuts=(), held_as=jnp.bfloat16):
    level = levels(key, shape, cuts, -0.22, 0.18) if cuts else 1.0
    drawn = jax.random.normal(key, shape, jnp.float32) * scale * level
    return jnp.minimum(jnp.maximum(drawn, -reach), reach).astype(held_as)


def bell_draw_with(key, dims, spread, bound, pieces, heavy, kind=jnp.bfloat16):
    drawn = spread * jax.random.normal(key, dims, jnp.float32)
    if pieces:
        drawn = drawn * levels(key, dims, pieces, -0.22, 0.18)
    return jnp.clip(with_spikes(drawn, jax.random.fold_in(key, 3), *heavy), -bound, bound).astype(kind)


def setup_inputs(seed: int = 0) -> dict:
    arg_keys = jax.random.split(jax.random.key(seed), 5)
    primal = centred(arg_keys[0], (MP, NPTS), 1.0, 6.0, ((0, 16), (1, 16)))
    adjoint_pencils = bell_draw_with(arg_keys[1], (MA, NPTS), NPTS ** -0.5, 0.01953125, ((0, 16), (1, 16)), (1, 0, 16, 2.0))
    weights = jnp.clip(jnp.exp(math.log(2.0) - 2.3025851 * jax.random.uniform(arg_keys[2], (NPTS,), jnp.float32) ** levels(arg_keys[2], (NPTS,), ((0, 16),), -0.2, 0.2)), 0.2, 2.0)
    pencil_map = draw_pencil_map(jax.random.fold_in(arg_keys[4], 71), 0)
    return {"primal": primal, "adjoint_pencils": adjoint_pencils, "weights": weights, "pencil_map": pencil_map}


def reference(primal, adjoint_pencils, weights, pencil_map):
    weighted = (primal.astype(jnp.float32) * weights[None, :]).astype(jnp.bfloat16)
    blocks = adjoint_pencils.reshape(MA, PENCILS, PEN_LEN)
    tiled = jnp.zeros_like(blocks).at[:, pencil_map, :].set(blocks).reshape(MA, NPTS)
    return lax.dot_general(tiled, weighted, (((1,), (1,)), ((), ())), preferred_element_type=jnp.float32)
```

```python
import functools
import jax
import jax.numpy as jnp
from jax import lax
from jax.experimental import pallas as pl
from jax.experimental.pallas import tpu as pltpu
from jax.sharding import PartitionSpec as P

PEN = 128
NX, NZ = 4, 8
TILES = 16
DEV_PEN = 96
SHARE = 6
MESH = pl.DeviceIdType.MESH
BLK = SHARE * PEN
KLOC = 4 * BLK


def where_am_i():
    space = lax.axis_index("space")
    snap = lax.axis_index("snap")
    return space // 2, space % 2, snap // 8, (snap // 2) % NX, snap % 2


def device(z, ylo, yh, x, c):
    return {"space": z * 2 + ylo, "snap": yh * 8 + x * 2 + c}


def sort_kernel(pos_a, pos_p, a_ref, p_ref, w_ref, as_ref, ps_ref):
    for i in range(DEV_PEN):
        at = pos_a[0, i]
        lane = pl.ds(pl.multiple_of((at % SHARE) * PEN, PEN), PEN)
        as_ref[at // SHARE, :, lane] = a_ref[:, i * PEN:(i + 1) * PEN]
    for i in range(DEV_PEN):
        at = pos_p[0, i]
        lane = pl.ds(pl.multiple_of((at % 24) * PEN, PEN), PEN)
        span = slice(i * PEN, (i + 1) * PEN)
        ps_ref[at // 24, :, lane] = (p_ref[:, span].astype(jnp.float32) * w_ref[:, span]).astype(jnp.bfloat16)


def sort_local(primal, adjoint, weights, pencil_map):
    z, ylo, _, _, _ = where_am_i()
    space = lax.axis_index("space")
    maps = pencil_map.reshape(TILES, DEV_PEN)
    target = maps // DEV_PEN
    before = jnp.arange(DEV_PEN)[None, :] < jnp.arange(DEV_PEN)[:, None]
    rank = jnp.sum((target[:, :, None] == target[:, None, :]) & before[None], axis=2, dtype=jnp.int32)
    own_target = lax.dynamic_index_in_dim(target, space, 0, keepdims=False)
    own_rank = lax.dynamic_index_in_dim(rank, space, 0, keepdims=False)
    dz_a = (own_target // 2 - z) % NZ
    pos_a = (dz_a * 2 + own_target % 2) * SHARE + own_rank
    src = jnp.arange(TILES, dtype=jnp.int32)
    dz_p = (z - src // 2) % NZ
    base = (dz_p % NX) * 24 + (dz_p // NX) * 12 + (src % 2) * SHARE
    place = base[:, None] + rank
    slots = space * DEV_PEN + jnp.arange(DEV_PEN, dtype=jnp.int32)
    pos_p = jnp.sum(jnp.where(maps[None] == slots[:, None, None], place[None], 0), axis=(1, 2), dtype=jnp.int32)
    rows_a, points = adjoint.shape
    rows_p = primal.shape[0]
    steps = 4
    return pl.pallas_call(
        sort_kernel,
        grid=(steps,),
        in_specs=[
            pl.BlockSpec(memory_space=pltpu.SMEM),
            pl.BlockSpec(memory_space=pltpu.SMEM),
            pl.BlockSpec((rows_a // steps, points), lambda i: (i, 0)),
            pl.BlockSpec((rows_p // steps, points), lambda i: (i, 0)),
            pl.BlockSpec((1, points), lambda i: (0, 0)),
        ],
        out_specs=[
            pl.BlockSpec((TILES, rows_a // steps, BLK), lambda i: (0, i, 0)),
            pl.BlockSpec((NX, rows_p // steps, KLOC), lambda i: (0, i, 0)),
        ],
        out_shape=[
            jax.ShapeDtypeStruct((TILES, rows_a, BLK), jnp.bfloat16),
            jax.ShapeDtypeStruct((NX, rows_p, KLOC), jnp.bfloat16),
        ],
        name="sort_local",
    )(pos_a[None], pos_p[None], adjoint, primal, weights[None])


ORDER = (0, 1, 7, 2, 6, 3, 5, 4)


def main_kernel(as_ref, ps_ref, o_ref, r1, afin, pfin, own, psend, rx, tot, r2,
                ss1, rs1, ssp, rsp, ssy, rsy, ssc, rsc, ssx, rsx, ss2, rs2):
    z, ylo, yh, x, c = where_am_i()
    space = z * 2 + ylo

    def remote(src, dst, ss, rs, dev):
        return pltpu.make_async_remote_copy(src_ref=src, dst_ref=dst, send_sem=ss, recv_sem=rs,
                                            device_id=dev, device_id_type=MESH)

    bar = pltpu.get_barrier_semaphore()

    def greet(dev):
        pl.semaphore_signal(bar, inc=1, device_id=dev, device_id_type=MESH)

    for zi in range(2):
        for xs in range(NX):
            dev = device((z - x - 4 * zi + 2 * NZ) % NZ, ylo, yh, xs, c)
            if zi == 0 and xs == 0:
                @pl.when(x != 0)
                def _():
                    greet(dev)
            else:
                greet(dev)
    for d in range(1, NX):
        greet(device(z, ylo, yh, (x + d) % NX, c))
    greet(device(z, ylo, 1 - yh, x, c))
    greet(device(z, 1 - ylo, 0, x, c))
    greet(device(z, 1 - ylo, 1, x, c))
    greet(device(z, ylo, yh, x, 1 - c))
    for d in range(1, TILES):
        to = (space + d) % TILES
        greet(device(to // 2, to % 2, yh, x, c))
    pl.semaphore_wait(bar, 7 + 3 + 3 + 1 + 15 + (x + NX - 1) // NX)

    def a_copy(dz):
        return remote(as_ref.at[pl.ds(dz * 2, 2)], r1.at[dz // NX, x], ss1.at[dz], rs1.at[dz // NX, x],
                      device((z + dz) % NZ, ylo, yh, dz % NX, c))

    local_a = pltpu.make_async_copy(as_ref.at[pl.ds(0, 2)], r1.at[0, 0], rs1.at[0, 0])
    for dz in ORDER:
        if dz == 0:
            @pl.when(x == 0)
            def _():
                local_a.start()

            @pl.when(x != 0)
            def _():
                a_copy(0).start()
        else:
            a_copy(dz).start()

    own_p = pltpu.make_async_copy(ps_ref.at[x], pfin.at[0], rsp.at[0])
    own_p.start()
    p_copies = []
    for d in (1, 3, 2):
        cp = remote(ps_ref.at[(x + d) % NX], pfin.at[(NX - d)], ssp.at[d - 1], rsp.at[NX - d],
                    device(z, ylo, yh, (x + d) % NX, c))
        cp.start()
        p_copies.append(cp)

    chunks = [(zi, d) for zi in range(2) for d in range(NX)]

    def y_copies(k, local=True):
        zi, d = chunks[k]
        xs = (x + d) % NX
        rb = yh * 8 + xs * 2 + c
        dst = afin.at[rb, :, pl.ds(pl.multiple_of((zi * 2 + ylo) * BLK, BLK), BLK)]
        mine = r1.at[zi, xs, ylo]
        other = r1.at[zi, xs, 1 - ylo]
        rs = rsy.at[yh, xs, zi, ylo]
        out = [
            remote(other, dst, ssy.at[k, 0], rs, device(z, 1 - ylo, yh, x, c)),
            remote(other, dst, ssy.at[k, 1], rs, device(z, 1 - ylo, 1 - yh, x, c)),
            remote(mine, dst, ssy.at[k, 2], rs, device(z, ylo, 1 - yh, x, c)),
        ]
        return out + ([pltpu.make_async_copy(mine, dst, rs)] if local else [])

    def blocks(k, core):
        zi, d = chunks[k]
        xs = (x + d) % NX
        for dy in range(2):
            for dl in range(2):
                ys, ls = (yh + dy) % 2, (ylo + dl) % 2
                rb = ys * 8 + xs * 2 + core
                blk = afin.at[rb, :, pl.ds(pl.multiple_of((zi * 2 + ls) * BLK, BLK), BLK)]
                yield blk, (ys, xs, zi, ls), (k, dy, dl)

    def c_copies(k):
        return [remote(blk, blk, ssc.at[send], rsc.at[at], device(z, ylo, yh, x, 1 - c))
                for blk, at, send in blocks(k, c)]

    lag = 2
    for k in range(len(chunks) + lag):
        if k < len(chunks):
            zi, d = chunks[k]
            xs = (x + d) % NX
            pltpu.make_async_copy(as_ref.at[pl.ds(0, 2)], r1.at[zi, xs], rs1.at[zi, xs]).wait()
            for cp in y_copies(k):
                cp.start()
        if k >= lag:
            for (blk, at, _), cp in zip(blocks(k - lag, c), c_copies(k - lag)):
                pltpu.make_async_copy(blk, blk, rsy.at[at]).wait()
                cp.start()
    for k in range(len(chunks)):
        for blk, at, _ in blocks(k, 1 - c):
            pltpu.make_async_copy(blk, blk, rsc.at[at]).wait()

    rows_mm = 256

    def product(slot, put):
        def body(i, carry):
            at = pl.multiple_of(i * (rows_mm // 64), rows_mm // 64)
            a = afin[pl.ds(at, rows_mm // 64)].reshape(rows_mm, KLOC)
            put(pl.multiple_of(i * rows_mm, rows_mm), lax.dot_general(
                a, pfin[slot], (((1,), (1,)), ((), ())), preferred_element_type=jnp.float32))
            return carry
        lax.fori_loop(0, 1024 // rows_mm, body, 0)

    def put_own(row, v):
        own[pl.ds(row, rows_mm), :] = v

    x_copies = []
    own_p.wait()
    product(0, put_own)
    for d in (1, 3, 2):
        pltpu.make_async_copy(ps_ref.at[0], pfin.at[d], rsp.at[d]).wait()

        def put_send(row, v, d=d):
            psend[d - 1, pl.ds(row, rows_mm), :] = v.astype(psend.dtype)
        product(d, put_send)
        cp = remote(psend.at[d - 1], rx.at[NX - d - 1], ssx.at[d - 1], rsx.at[NX - d - 1],
                    device(z, ylo, yh, (x + d) % NX, c))
        cp.start()
        x_copies.append(cp)

    for d in range(1, NX):
        pltpu.make_async_copy(psend.at[0], rx.at[d - 1], rsx.at[d - 1]).wait()
    tot[...] = (own[...] + rx[0].astype(jnp.float32) + rx[1].astype(jnp.float32)
                + rx[2].astype(jnp.float32)).reshape(tot.shape)

    f_copies = []
    for d in range(1, TILES):
        to = (space + d) % TILES
        cp = remote(tot.at[to], r2.at[TILES - d - 1], ss2.at[d - 1], rs2.at[TILES - d - 1],
                    device(to // 2, to % 2, yh, x, c))
        cp.start()
        f_copies.append(cp)
    acc = tot[space]
    for d in range(1, TILES):
        pltpu.make_async_copy(tot.at[0], r2.at[d - 1], rs2.at[d - 1]).wait()
        acc = acc + r2[d - 1]
    o_ref[...] = acc

    @pl.when(x != 0)
    def _():
        a_copy(0).wait_send()
    for dz in range(1, NZ):
        a_copy(dz).wait_send()
    for cp in p_copies + x_copies + f_copies:
        cp.wait_send()
    for k in range(len(chunks)):
        for cp in y_copies(k, local=False):
            cp.wait_send()
        for cp in c_copies(k):
            cp.wait_send()


def exchange(a_sorted, p_sorted):
    bf, f32 = jnp.bfloat16, jnp.float32
    dma = pltpu.SemaphoreType.DMA
    return pl.pallas_call(
        main_kernel,
        in_specs=[pl.BlockSpec(memory_space=pl.ANY)] * 2,
        out_specs=pl.BlockSpec(memory_space=pltpu.VMEM),
        out_shape=jax.ShapeDtypeStruct((64, 128), f32),
        scratch_shapes=[
            pltpu.VMEM((2, NX, 2, 64, BLK), bf),
            pltpu.VMEM((16, 64, KLOC), bf),
            pltpu.VMEM((NX, 128, KLOC), bf),
            pltpu.VMEM((1024, 128), f32),
            pltpu.VMEM((3, 1024, 128), bf),
            pltpu.VMEM((3, 1024, 128), bf),
            pltpu.VMEM((TILES, 64, 128), f32),
            pltpu.VMEM((TILES - 1, 64, 128), f32),
            dma((NZ,)), dma((2, NX)),
            dma((3,)), dma((NX,)),
            dma((8, 3)), dma((2, NX, 2, 2)),
            dma((8, 2, 2)), dma((2, NX, 2, 2)),
            dma((3,)), dma((3,)),
            dma((TILES - 1,)), dma((TILES - 1,)),
        ],
        compiler_params=pltpu.CompilerParams(
            collective_id=0, has_side_effects=True, vmem_limit_bytes=48 * 1024 * 1024),
        name="exchange",
    )(a_sorted, p_sorted)


def on_device(primal, adjoint_pencils, weights, pencil_map):
    a_sorted, p_sorted = sort_local(primal, adjoint_pencils, weights, pencil_map)
    return exchange(a_sorted, p_sorted)


def solution(mesh):
    placed = (P("snap", "space"), P("snap", "space"), P("space"), P())
    return jax.shard_map(
        on_device, mesh=mesh, in_specs=placed, out_specs=P("space", "snap"), check_vma=False
    )
```

```python
import functools
import jax
import jax.numpy as jnp
from jax import lax
from jax.experimental import pallas as pl
from jax.experimental.pallas import tpu as pltpu
from jax.sharding import PartitionSpec as P

PEN = 128
NX, NZ = 4, 8
TILES = 16
DEV_PEN = 96
SHARE = 6
MESH = pl.DeviceIdType.MESH
BLK = SHARE * PEN
KLOC = 4 * BLK


def where_am_i():
    space = lax.axis_index("space")
    snap = lax.axis_index("snap")
    return space // 2, space % 2, snap // 8, (snap // 2) % NX, snap % 2


def device(z, ylo, yh, x, c):
    return {"space": z * 2 + ylo, "snap": yh * 8 + x * 2 + c}


ORDER = (0, 1, 7, 2, 6, 4, 3, 5)
XORDER = (1, 3, 2)
ROWS = 256
STEPS = 1024 // ROWS


def main_kernel(idx_a, idx_p, w_ref, a_hbm, p_hbm, o_ref, a_v, p_v, asort, psort, r1, afin, pfin,
                own, psend, rx, tot, r2,
                lsem, ss1, rs1, ssp, rsp, ssy, rsy, ssc, rsc, ssx, rsx, ss2, rs2):
    z, ylo, yh, x, c = where_am_i()
    space = z * 2 + ylo

    def remote(src, dst, ss, rs, dev):
        return pltpu.make_async_remote_copy(src_ref=src, dst_ref=dst, send_sem=ss, recv_sem=rs,
                                            device_id=dev, device_id_type=MESH)

    def arrived(ref, sem):
        pltpu.make_async_copy(ref, ref, sem).wait()

    def load(hbm, v, sem):
        def body(i, carry):
            lane = pl.ds(pl.multiple_of(i * PEN, PEN), PEN)
            pltpu.make_async_copy(hbm.at[:, lane], v.at[i], sem).start()
            return carry
        lax.fori_loop(0, DEV_PEN, body, 0)

    load(a_hbm, a_v, lsem.at[0])

    bar = pltpu.get_barrier_semaphore()

    def greet(dev):
        pl.semaphore_signal(bar, inc=1, device_id=dev, device_id_type=MESH)

    for zi in range(2):
        for xs in range(NX):
            dev = device((z - x - 4 * zi + 2 * NZ) % NZ, ylo, yh, xs, c)
            if zi == 0 and xs == 0:
                @pl.when(x != 0)
                def _():
                    greet(dev)
            else:
                greet(dev)
    for d in range(1, NX):
        greet(device(z, ylo, yh, (x + d) % NX, c))
    greet(device(z, ylo, 1 - yh, x, c))
    greet(device(z, 1 - ylo, 0, x, c))
    greet(device(z, 1 - ylo, 1, x, c))
    greet(device(z, ylo, yh, x, 1 - c))
    for d in range(1, TILES):
        to = (space + d) % TILES
        greet(device(to // 2, to % 2, yh, x, c))

    load(p_hbm, p_v, lsem.at[1])

    arrived(a_v, lsem.at[0])
    for dz in range(NZ):
        for lt in range(2):
            t = ((z + dz) % NZ) * 2 + lt
            for r in range(SHARE):
                asort[dz, lt, :, r * PEN:(r + 1) * PEN] = a_v[idx_a[t, r]]

    pl.semaphore_wait(bar, 7 + 3 + 3 + 1 + 15 + (x + NX - 1) // NX)

    def a_copy(dz, l):
        lt = (1 - ylo + l) % 2
        return remote(asort.at[dz, lt], r1.at[dz // NX, x, lt], ss1.at[dz, l], rs1.at[dz // NX, x, lt],
                      device((z + dz) % NZ, ylo, yh, dz % NX, c))

    for dz in ORDER:
        for l in range(2):
            if dz == 0:
                lt = (1 - ylo + l) % 2

                @pl.when(x == 0)
                def _():
                    pltpu.make_async_copy(asort.at[0, lt], r1.at[0, 0, lt], rs1.at[0, 0, lt]).start()

                @pl.when(x != 0)
                def _():
                    a_copy(0, l).start()
            else:
                a_copy(dz, l).start()

    def p_copy(slot):
        d = XORDER[slot - 1]
        return remote(psort.at[d], pfin.at[XORDER.index(NX - d) + 1], ssp.at[slot - 1],
                      rsp.at[XORDER.index(NX - d) + 1], device(z, ylo, yh, (x + d) % NX, c))

    own_p = pltpu.make_async_copy(psort.at[0], pfin.at[0], rsp.at[0])
    arrived(p_v, lsem.at[1])
    for step, d in enumerate(XORDER + (0,)):
        for zi in range(2):
            dz = (x + d) % NX + NX * zi
            for ls in range(2):
                src = ((z - dz + NZ) % NZ) * 2 + ls
                for r in range(SHARE):
                    i = idx_p[src, r]
                    at = ((zi * 2 + ls) * SHARE + r) * PEN
                    psort[d, :, at:at + PEN] = (
                        p_v[i].astype(jnp.float32) * w_ref[i]).astype(jnp.bfloat16)
        if step >= 1:
            p_copy(step).start()
    own_p.start()

    flip = x // 3
    chunks = [(j, d, l) for j in range(2) for d in (0, 1, 3, 2) for l in range(2)]

    def chunk(k):
        j, d, l = chunks[k]
        return (j + flip) % 2, (x + d) % NX, (1 - ylo + l) % 2

    def block(ys, xs, core, zi, ls):
        return afin.at[ys * 8 + xs * 2 + core, :, pl.ds(pl.multiple_of((zi * 2 + ls) * BLK, BLK), BLK)]

    def y_copies(k):
        zi, xs, lt = chunk(k)
        src = r1.at[zi, xs, lt]
        dst = block(yh, xs, c, zi, ylo)
        rs = rsy.at[yh, xs, zi, ylo]
        out = [remote(src, dst, ssy.at[k, 0], rs, device(z, lt, 1 - yh, x, c))]
        if chunks[k][2] == 0:
            out.append(remote(src, dst, ssy.at[k, 1], rs, device(z, lt, yh, x, c)))
        return out

    def sources(k):
        j, d, l = chunks[k]
        zi, xs = (j + flip) % 2, (x + d) % NX
        ls = (ylo + 1 - l) % 2
        return [((yh + dy) % 2, xs, zi, ls, dy) for dy in range(2)]

    def c_copies(k):
        return [remote(block(ys, xs, c, zi, ls), block(ys, xs, c, zi, ls), ssc.at[k, dy],
                       rsc.at[ys, xs, zi, ls], device(z, ylo, yh, x, 1 - c))
                for ys, xs, zi, ls, dy in sources(k)]

    lag = 4
    for k in range(len(chunks) + lag):
        if k < len(chunks):
            zi, xs, lt = chunk(k)
            arrived(r1.at[zi, xs, lt], rs1.at[zi, xs, lt])
            for cp in y_copies(k):
                cp.start()
            if chunks[k][2] == 1:
                pltpu.make_async_copy(r1.at[zi, xs, lt], block(yh, xs, c, zi, ylo),
                                      rsy.at[yh, xs, zi, ylo]).start()
        if k >= lag:
            for (ys, xs, zi, ls, _), cp in zip(sources(k - lag), c_copies(k - lag)):
                arrived(block(ys, xs, c, zi, ls), rsy.at[ys, xs, zi, ls])
                cp.start()
    for k in range(len(chunks)):
        for ys, xs, zi, ls, _ in sources(k):
            arrived(block(ys, xs, 1 - c, zi, ls), rsc.at[ys, xs, zi, ls])

    first = z // 2

    def rows_at(i):
        return (first + i) % STEPS

    def lhs(i):
        return afin[pl.ds(rows_at(i) * (ROWS // 64), ROWS // 64)].reshape(ROWS, KLOC)

    def times(a, b):
        return lax.dot_general(a, b, (((1,), (1,)), ((), ())), preferred_element_type=jnp.float32)

    def x_copy(slot, i):
        d = XORDER[slot - 1]
        back = XORDER.index(NX - d)
        return remote(psend.at[slot - 1, rows_at(i)], rx.at[back, rows_at(i)], ssx.at[slot - 1, i],
                      rsx.at[back, i], device(z, ylo, yh, (x + d) % NX, c))

    arrived(pfin.at[0], rsp.at[0])
    arrived(pfin.at[1], rsp.at[1])
    for i in range(STEPS):
        v = times(lhs(i), pfin[0:2].reshape(256, KLOC))
        own[rows_at(i)] = v[:, :128]
        psend[0, rows_at(i)] = v[:, 128:].astype(psend.dtype)
        x_copy(1, i).start()
    for slot in (2, 3):
        arrived(pfin.at[slot], rsp.at[slot])
        for i in range(STEPS):
            psend[slot - 1, rows_at(i)] = times(lhs(i), pfin[slot]).astype(psend.dtype)
            x_copy(slot, i).start()

    def f_copy(i, j):
        to = rows_at(i) * (ROWS // 64) + j
        return to, remote(tot.at[to], r2.at[space], ss2.at[i, j], rs2.at[space],
                          device(to // 2, to % 2, yh, x, c))

    for i in range(STEPS):
        at = rows_at(i)
        total = own[at]
        for slot in range(3):
            arrived(rx.at[slot, at], rsx.at[slot, i])
            total = total + rx[slot, at].astype(jnp.float32)
        tot[pl.ds(at * (ROWS // 64), ROWS // 64)] = total.reshape(ROWS // 64, 64, 128)
        for j in range(ROWS // 64):
            to = at * (ROWS // 64) + j

            @pl.when(to != space)
            def _():
                f_copy(i, j)[1].start()
    acc = tot[space]
    for d in range(1, TILES):
        frm = (space + d) % TILES
        arrived(r2.at[frm], rs2.at[frm])
        acc = acc + r2[frm]
    o_ref[...] = acc

    for l in range(2):
        @pl.when(x != 0)
        def _():
            a_copy(0, l).wait_send()
        for dz in range(1, NZ):
            a_copy(dz, l).wait_send()
    for slot in range(1, NX):
        p_copy(slot).wait_send()
        for i in range(STEPS):
            x_copy(slot, i).wait_send()
    for k in range(len(chunks)):
        for cp in y_copies(k) + c_copies(k):
            cp.wait_send()
    for i in range(STEPS):
        for j in range(ROWS // 64):
            to = rows_at(i) * (ROWS // 64) + j

            @pl.when(to != space)
            def _():
                f_copy(i, j)[1].wait_send()


def exchange(idx_a, idx_p, weights, adjoint, primal):
    bf, f32 = jnp.bfloat16, jnp.float32
    dma = pltpu.SemaphoreType.DMA
    smem = pl.BlockSpec(memory_space=pltpu.SMEM)
    hbm = pl.BlockSpec(memory_space=pl.ANY)
    vmem = pl.BlockSpec(memory_space=pltpu.VMEM)
    return pl.pallas_call(
        main_kernel,
        in_specs=[smem, smem, vmem, hbm, hbm],
        out_specs=vmem,
        out_shape=jax.ShapeDtypeStruct((64, 128), f32),
        scratch_shapes=[
            pltpu.VMEM((DEV_PEN, 64, PEN), bf),
            pltpu.VMEM((DEV_PEN, 128, PEN), bf),
            pltpu.VMEM((NZ, 2, 64, BLK), bf),
            pltpu.VMEM((NX, 128, KLOC), bf),
            pltpu.VMEM((2, NX, 2, 64, BLK), bf),
            pltpu.VMEM((16, 64, KLOC), bf),
            pltpu.VMEM((NX, 128, KLOC), bf),
            pltpu.VMEM((STEPS, ROWS, 128), f32),
            pltpu.VMEM((3, STEPS, ROWS, 128), bf),
            pltpu.VMEM((3, STEPS, ROWS, 128), bf),
            pltpu.VMEM((TILES, 64, 128), f32),
            pltpu.VMEM((TILES, 64, 128), f32),
            dma((2,)),
            dma((NZ, 2)), dma((2, NX, 2)),
            dma((3,)), dma((NX,)),
            dma((16, 2)), dma((2, NX, 2, 2)),
            dma((16, 2)), dma((2, NX, 2, 2)),
            dma((3, STEPS)), dma((3, STEPS)),
            dma((STEPS, ROWS // 64)), dma((TILES,)),
        ],
        compiler_params=pltpu.CompilerParams(
            collective_id=0, has_side_effects=True, vmem_limit_bytes=60 * 1024 * 1024),
        name="exchange",
    )(idx_a, idx_p, weights.reshape(DEV_PEN, 1, PEN), adjoint, primal)


def on_device(primal, adjoint_pencils, weights, pencil_map):
    space = lax.axis_index("space")
    maps = pencil_map.reshape(TILES, DEV_PEN)
    target = maps // DEV_PEN
    before = jnp.arange(DEV_PEN)[None, :] < jnp.arange(DEV_PEN)[:, None]
    rank = jnp.sum((target[:, :, None] == target[:, None, :]) & before[None], axis=2, dtype=jnp.int32)
    of_rank = jnp.arange(SHARE, dtype=jnp.int32)[None, :, None]
    here = (target == space)[:, None, :] & (rank[:, None, :] == of_rank)
    idx_p = jnp.sum(jnp.where(here, maps[:, None, :] - space * DEV_PEN, 0), axis=2, dtype=jnp.int32)
    own_target = lax.dynamic_index_in_dim(target, space, 0, keepdims=True)
    own_rank = lax.dynamic_index_in_dim(rank, space, 0, keepdims=True)
    to = (own_target == jnp.arange(TILES, dtype=jnp.int32)[:, None])[:, None, :] & (own_rank[:, None, :] == of_rank)
    idx_a = jnp.sum(jnp.where(to, jnp.arange(DEV_PEN, dtype=jnp.int32), 0), axis=2, dtype=jnp.int32)
    return exchange(idx_a, idx_p, weights, adjoint_pencils, primal)


def solution(mesh):
    placed = (P("snap", "space"), P("snap", "space"), P("space"), P())
    return jax.shard_map(
        on_device, mesh=mesh, in_specs=placed, out_specs=P("space", "snap"), check_vma=False
    )
```

```python
import functools
import jax
import jax.numpy as jnp
from jax import lax
from jax.experimental import pallas as pl
from jax.experimental.pallas import tpu as pltpu
from jax.sharding import PartitionSpec as P

PEN = 128
NX, NZ = 4, 8
TILES = 16
DEV_PEN = 96
SHARE = 6
MESH = pl.DeviceIdType.MESH
BLK = SHARE * PEN
KLOC = 4 * BLK


def where_am_i():
    space = lax.axis_index("space")
    snap = lax.axis_index("snap")
    return space // 2, space % 2, snap // 8, (snap // 2) % NX, snap % 2


def device(z, ylo, yh, x, c):
    return {"space": z * 2 + ylo, "snap": yh * 8 + x * 2 + c}


ORDER = (0, 1, 7, 2, 6, 4, 3, 5)
XORDER = (1, 3, 2)
ROWS = 256
STEPS = 1024 // ROWS


def main_kernel(idx_a, idx_p, w_ref, a_hbm, p_hbm, o_ref, a_v, p_v, asort, psort, r1, afin, pfin,
                own, psend, rx, tot, r2,
                lsem, ss1, rs1, ssp, rsp, ssy, rsy, ssc, rsc, ssx, rsx, ss2, rs2):
    z, ylo, yh, x, c = where_am_i()
    space = z * 2 + ylo

    def remote(src, dst, ss, rs, dev):
        return pltpu.make_async_remote_copy(src_ref=src, dst_ref=dst, send_sem=ss, recv_sem=rs,
                                            device_id=dev, device_id_type=MESH)

    def arrived(ref, sem):
        pltpu.make_async_copy(ref, ref, sem).wait()

    def load(hbm, v, sem):
        def body(i, carry):
            lane = pl.ds(pl.multiple_of(i * PEN, PEN), PEN)
            pltpu.make_async_copy(hbm.at[:, lane], v.at[i], sem).start()
            return carry
        lax.fori_loop(0, DEV_PEN, body, 0)

    load(a_hbm, a_v, lsem.at[0])

    bar = pltpu.get_barrier_semaphore()

    def greet(dev):
        pl.semaphore_signal(bar, inc=1, device_id=dev, device_id_type=MESH)

    for zi in range(2):
        for xs in range(NX):
            dev = device((z - x - 4 * zi + 2 * NZ) % NZ, ylo, yh, xs, c)
            if zi == 0 and xs == 0:
                @pl.when(x != 0)
                def _():
                    greet(dev)
            else:
                greet(dev)
    for d in range(1, NX):
        greet(device(z, ylo, yh, (x + d) % NX, c))
    greet(device(z, ylo, 1 - yh, x, c))
    greet(device(z, 1 - ylo, 0, x, c))
    greet(device(z, 1 - ylo, 1, x, c))
    greet(device(z, ylo, yh, x, 1 - c))
    for d in range(1, TILES):
        to = (space + d) % TILES
        greet(device(to // 2, to % 2, yh, x, c))

    arrived(a_v, lsem.at[0])
    for dz in range(NZ):
        for lt in range(2):
            t = ((z + dz) % NZ) * 2 + lt
            for r in range(SHARE):
                v = a_v[idx_a[r, t]]
                for h in range(2):
                    asort[dz, lt, h, :, r * PEN:(r + 1) * PEN] = v[h * 32:(h + 1) * 32]

    pl.semaphore_wait(bar, 7 + 3 + 3 + 1 + 15 + (x + NX - 1) // NX)

    def a_copy(h, dz, l):
        lt = (1 - ylo + l) % 2
        return remote(asort.at[dz, lt, h], r1.at[dz // NX, x, lt, h], ss1.at[dz, l, h],
                      rs1.at[dz // NX, x, lt, h], device((z + dz) % NZ, ylo, yh, dz % NX, c))

    for h in range(2):
        for dz in ORDER:
            for l in range(2):
                if dz == 0:
                    lt = (1 - ylo + l) % 2

                    @pl.when(x == 0)
                    def _():
                        pltpu.make_async_copy(asort.at[0, lt, h], r1.at[0, 0, lt, h], rs1.at[0, 0, lt, h]).start()

                    @pl.when(x != 0)
                    def _():
                        a_copy(h, 0, l).start()
                else:
                    a_copy(h, dz, l).start()
    load(p_hbm, p_v, lsem.at[1])

    def p_copy(slot):
        d = XORDER[slot - 1]
        return remote(psort.at[d], pfin.at[XORDER.index(NX - d) + 1], ssp.at[slot - 1],
                      rsp.at[XORDER.index(NX - d) + 1], device(z, ylo, yh, (x + d) % NX, c))

    own_p = pltpu.make_async_copy(psort.at[0], pfin.at[0], rsp.at[0])
    arrived(p_v, lsem.at[1])
    for step, d in enumerate(XORDER + (0,)):
        for zi in range(2):
            dz = (x + d) % NX + NX * zi
            for ls in range(2):
                src = ((z - dz + NZ) % NZ) * 2 + ls
                for r in range(SHARE):
                    i = idx_p[r, src]
                    at = ((zi * 2 + ls) * SHARE + r) * PEN
                    psort[d, :, at:at + PEN] = (
                        p_v[i].astype(jnp.float32) * w_ref[i]).astype(jnp.bfloat16)
        if step >= 1:
            p_copy(step).start()
    own_p.start()

    flip = x // 3
    chunks = [(h, j, d, l) for h in range(2) for j in range(2) for d in (0, 1, 3, 2) for l in range(2)]

    def block(h, ys, xs, core, zi, ls):
        lane = pl.ds(pl.multiple_of((zi * 2 + ls) * BLK, BLK), BLK)
        return afin.at[h, ys * 8 + xs * 2 + core, :, lane]

    def y_copies(k):
        h, j, d, l = chunks[k]
        zi, xs, lt = (j + flip) % 2, (x + d) % NX, (1 - ylo + l) % 2
        src = r1.at[zi, xs, lt, h]
        dst = block(h, yh, xs, c, zi, ylo)
        rs = rsy.at[h, yh, xs, zi, ylo]
        out = [remote(src, dst, ssy.at[k, 0], rs, device(z, lt, 1 - yh, x, c))]
        if l == 0:
            out.append(remote(src, dst, ssy.at[k, 1], rs, device(z, lt, yh, x, c)))
        return src, rs1.at[zi, xs, lt, h], out, dst, rs

    def sources(k):
        h, j, d, l = chunks[k]
        zi, xs = (j + flip) % 2, (x + d) % NX
        ls = (ylo + 1 - l) % 2
        return [(h, (yh + dy) % 2, xs, zi, ls, dy) for dy in range(2)]

    def c_copies(k):
        return [remote(block(h, ys, xs, c, zi, ls), block(h, ys, xs, c, zi, ls), ssc.at[k, dy],
                       rsc.at[h, ys, xs, zi, ls], device(z, ylo, yh, x, 1 - c))
                for h, ys, xs, zi, ls, dy in sources(k)]

    lag = 6
    for k in range(len(chunks) + lag):
        if k < len(chunks):
            src, sem, out, dst, rs = y_copies(k)
            arrived(src, sem)
            for cp in out:
                cp.start()
            if chunks[k][3] == 1:
                pltpu.make_async_copy(src, dst, rs).start()
        if k >= lag:
            for (h, ys, xs, zi, ls, _), cp in zip(sources(k - lag), c_copies(k - lag)):
                arrived(block(h, ys, xs, c, zi, ls), rsy.at[h, ys, xs, zi, ls])
                cp.start()
    for k in range(len(chunks)):
        for h, ys, xs, zi, ls, _ in sources(k):
            arrived(block(h, ys, xs, 1 - c, zi, ls), rsc.at[h, ys, xs, zi, ls])

    blocks = ROWS // 32

    def part(i):
        return i // 2, (z // 4 + i % 2) % 2 * blocks

    def lhs(i):
        h, at = part(i)
        return afin[h, pl.ds(at, blocks)].reshape(ROWS, KLOC)

    def times(a, b):
        return lax.dot_general(a, b, (((1,), (1,)), ((), ())), preferred_element_type=jnp.float32)

    def x_copy(slot, i):
        d = XORDER[slot - 1]
        back = XORDER.index(NX - d)
        return remote(psend.at[slot - 1, i], rx.at[back, i], ssx.at[slot - 1, i],
                      rsx.at[back, i], device(z, ylo, yh, (x + d) % NX, c))

    arrived(pfin.at[0], rsp.at[0])
    arrived(pfin.at[1], rsp.at[1])
    for i in range(STEPS):
        v = times(lhs(i), pfin[0:2].reshape(256, KLOC))
        own[i] = v[:, :128]
        psend[0, i] = v[:, 128:].astype(psend.dtype)
        x_copy(1, i).start()
    for slot in (2, 3):
        arrived(pfin.at[slot], rsp.at[slot])
        for i in range(STEPS):
            psend[slot - 1, i] = times(lhs(i), pfin[slot]).astype(psend.dtype)
            x_copy(slot, i).start()

    def f_copy(i, j):
        h, at = part(i)
        to = at + j
        return remote(tot.at[h, to], r2.at[h, space], ss2.at[i, j], rs2.at[h, space],
                      device(to // 2, to % 2, yh, x, c))

    for i in range(STEPS):
        h, at = part(i)
        total = own[i]
        for slot in range(3):
            arrived(rx.at[slot, i], rsx.at[slot, i])
            total = total + rx[slot, i].astype(jnp.float32)
        tot[h, pl.ds(at, blocks)] = total.reshape(blocks, 32, 128)
        for j in range(blocks):
            @pl.when(at + j != space)
            def _():
                f_copy(i, j).start()
    for h in range(2):
        acc = tot[h, space]
        for d in range(1, TILES):
            frm = (space + d) % TILES
            arrived(r2.at[h, frm], rs2.at[h, frm])
            acc = acc + r2[h, frm]
        o_ref[h * 32:(h + 1) * 32] = acc

    for h in range(2):
        for l in range(2):
            @pl.when(x != 0)
            def _():
                a_copy(h, 0, l).wait_send()
            for dz in range(1, NZ):
                a_copy(h, dz, l).wait_send()
    for slot in range(1, NX):
        p_copy(slot).wait_send()
        for i in range(STEPS):
            x_copy(slot, i).wait_send()
    for k in range(len(chunks)):
        for cp in y_copies(k)[2] + c_copies(k):
            cp.wait_send()
    for i in range(STEPS):
        for j in range(blocks):
            @pl.when(part(i)[1] + j != space)
            def _():
                f_copy(i, j).wait_send()


def exchange(idx_a, idx_p, weights, adjoint, primal):
    bf, f32 = jnp.bfloat16, jnp.float32
    dma = pltpu.SemaphoreType.DMA
    smem = pl.BlockSpec(memory_space=pltpu.SMEM)
    hbm = pl.BlockSpec(memory_space=pl.ANY)
    vmem = pl.BlockSpec(memory_space=pltpu.VMEM)
    return pl.pallas_call(
        main_kernel,
        in_specs=[smem, smem, vmem, hbm, hbm],
        out_specs=vmem,
        out_shape=jax.ShapeDtypeStruct((64, 128), f32),
        scratch_shapes=[
            pltpu.VMEM((DEV_PEN, 64, PEN), bf),
            pltpu.VMEM((DEV_PEN, 128, PEN), bf),
            pltpu.VMEM((NZ, 2, 2, 32, BLK), bf),
            pltpu.VMEM((NX, 128, KLOC), bf),
            pltpu.VMEM((2, NX, 2, 2, 32, BLK), bf),
            pltpu.VMEM((2, 16, 32, KLOC), bf),
            pltpu.VMEM((NX, 128, KLOC), bf),
            pltpu.VMEM((STEPS, ROWS, 128), f32),
            pltpu.VMEM((3, STEPS, ROWS, 128), bf),
            pltpu.VMEM((3, STEPS, ROWS, 128), bf),
            pltpu.VMEM((2, TILES, 32, 128), f32),
            pltpu.VMEM((2, TILES, 32, 128), f32),
            dma((2,)),
            dma((NZ, 2, 2)), dma((2, NX, 2, 2)),
            dma((3,)), dma((NX,)),
            dma((32, 2)), dma((2, 2, NX, 2, 2)),
            dma((32, 2)), dma((2, 2, NX, 2, 2)),
            dma((3, STEPS)), dma((3, STEPS)),
            dma((STEPS, ROWS // 32)), dma((2, TILES)),
        ],
        compiler_params=pltpu.CompilerParams(
            collective_id=0, has_side_effects=True, vmem_limit_bytes=60 * 1024 * 1024),
        name="exchange",
    )(idx_a.T, idx_p.T, weights.reshape(DEV_PEN, 1, PEN), adjoint, primal)


def on_device(primal, adjoint_pencils, weights, pencil_map):
    space = lax.axis_index("space")
    maps = pencil_map.reshape(TILES, DEV_PEN)
    target = maps // DEV_PEN
    before = jnp.arange(DEV_PEN)[None, :] < jnp.arange(DEV_PEN)[:, None]
    rank = jnp.sum((target[:, :, None] == target[:, None, :]) & before[None], axis=2, dtype=jnp.int32)
    of_rank = jnp.arange(SHARE, dtype=jnp.int32)[None, :, None]
    here = (target == space)[:, None, :] & (rank[:, None, :] == of_rank)
    idx_p = jnp.sum(jnp.where(here, maps[:, None, :] - space * DEV_PEN, 0), axis=2, dtype=jnp.int32)
    own_target = lax.dynamic_index_in_dim(target, space, 0, keepdims=True)
    own_rank = lax.dynamic_index_in_dim(rank, space, 0, keepdims=True)
    to = (own_target == jnp.arange(TILES, dtype=jnp.int32)[:, None])[:, None, :] & (own_rank[:, None, :] == of_rank)
    idx_a = jnp.sum(jnp.where(to, jnp.arange(DEV_PEN, dtype=jnp.int32), 0), axis=2, dtype=jnp.int32)
    return exchange(idx_a, idx_p, weights, adjoint_pencils, primal)


def solution(mesh):
    placed = (P("snap", "space"), P("snap", "space"), P("space"), P())
    return jax.shard_map(
        on_device, mesh=mesh, in_specs=placed, out_specs=P("space", "snap"), check_vma=False
    )
```

```python
import functools
import jax
import jax.numpy as jnp
from jax import lax
from jax.experimental import pallas as pl
from jax.experimental.pallas import tpu as pltpu
from jax.sharding import PartitionSpec as P

PEN = 128
NX, NZ = 4, 8
TILES = 16
DEV_PEN = 96
SHARE = 6
MESH = pl.DeviceIdType.MESH
BLK = SHARE * PEN
KLOC = 4 * BLK


def where_am_i():
    space = lax.axis_index("space")
    snap = lax.axis_index("snap")
    return space // 2, space % 2, snap // 8, (snap // 2) % NX, snap % 2


def device(z, ylo, yh, x, c):
    return {"space": z * 2 + ylo, "snap": yh * 8 + x * 2 + c}


ORDER = (0, 1, 7, 2, 6, 4, 3, 5)
XORDER = (1, 3, 2)
ROWS = 256
STEPS = 1024 // ROWS


def sort_kernel(idx_a, a_ref, o_ref):
    z, _, _, _, _ = where_am_i()
    for dz in range(NZ):
        for lt in range(2):
            t = ((z + dz) % NZ) * 2 + lt
            for r in range(SHARE):
                lane = pl.ds(pl.multiple_of(idx_a[r, t] * PEN, PEN), PEN)
                o_ref[0, dz, lt, :, r * PEN:(r + 1) * PEN] = a_ref[:, lane]


def sort_adjoint(idx_a, adjoint):
    rows, points = adjoint.shape
    return pl.pallas_call(
        sort_kernel,
        grid=(2,),
        in_specs=[pl.BlockSpec(memory_space=pltpu.SMEM),
                  pl.BlockSpec((rows // 2, points), lambda h: (h, 0))],
        out_specs=pl.BlockSpec((1, NZ, 2, rows // 2, BLK), lambda h: (h, 0, 0, 0, 0)),
        out_shape=jax.ShapeDtypeStruct((2, NZ, 2, rows // 2, BLK), jnp.bfloat16),
        name="sort_adjoint",
    )(idx_a, adjoint)


def main_kernel(idx_p, w_ref, asort, p_hbm, o_ref, p_v, psort, r1, afin, pfin,
                own, psend, rx, tot, fsend, r2,
                lsem, ss1, rs1, ssp, rsp, ssy, rsy, ssc, rsc, ssx, rsx, ss2, rs2):
    z, ylo, yh, x, c = where_am_i()
    space = z * 2 + ylo

    def remote(src, dst, ss, rs, dev):
        return pltpu.make_async_remote_copy(src_ref=src, dst_ref=dst, send_sem=ss, recv_sem=rs,
                                            device_id=dev, device_id_type=MESH)

    def arrived(ref, sem):
        pltpu.make_async_copy(ref, ref, sem).wait()

    def load(hbm, v, sem):
        def body(i, carry):
            lane = pl.ds(pl.multiple_of(i * PEN, PEN), PEN)
            pltpu.make_async_copy(hbm.at[:, lane], v.at[i], sem).start()
            return carry
        lax.fori_loop(0, DEV_PEN, body, 0)


    bar = pltpu.get_barrier_semaphore()

    def greet(dev):
        pl.semaphore_signal(bar, inc=1, device_id=dev, device_id_type=MESH)

    for zi in range(2):
        for xs in range(NX):
            dev = device((z - x - 4 * zi + 2 * NZ) % NZ, ylo, yh, xs, c)
            if zi == 0 and xs == 0:
                @pl.when(x != 0)
                def _():
                    greet(dev)
            else:
                greet(dev)
    for d in range(1, NX):
        greet(device(z, ylo, yh, (x + d) % NX, c))
    greet(device(z, ylo, 1 - yh, x, c))
    greet(device(z, 1 - ylo, 0, x, c))
    greet(device(z, 1 - ylo, 1, x, c))
    greet(device(z, ylo, yh, x, 1 - c))
    for d in range(1, TILES):
        to = (space + d) % TILES
        greet(device(to // 2, to % 2, yh, x, c))

    def p_copy(slot):
        d = XORDER[slot - 1]
        return remote(psort.at[d], pfin.at[XORDER.index(NX - d) + 1], ssp.at[slot - 1],
                      rsp.at[XORDER.index(NX - d) + 1], device(z, ylo, yh, (x + d) % NX, c))

    def sort_p(d):
        for zi in range(2):
            dz = (x + d) % NX + NX * zi
            for ls in range(2):
                src = ((z - dz + NZ) % NZ) * 2 + ls
                for r in range(SHARE):
                    i = idx_p[r, src]
                    at = ((zi * 2 + ls) * SHARE + r) * PEN
                    psort[d, :, at:at + PEN] = (
                        p_v[i].astype(jnp.float32) * w_ref[i]).astype(jnp.bfloat16)

    own_p = pltpu.make_async_copy(psort.at[0], pfin.at[0], rsp.at[0])
    load(p_hbm, p_v, lsem.at[0])
    arrived(p_v, lsem.at[0])
    sort_p(XORDER[0])

    pl.semaphore_wait(bar, 7 + 3 + 3 + 1 + 15 + (x + NX - 1) // NX)

    def a_copy(h, dz, l):
        lt = (1 - ylo + l) % 2
        return remote(asort.at[h, dz, lt], r1.at[dz // NX, x, lt, h], ss1.at[dz, l, h],
                      rs1.at[dz // NX, x, lt, h], device((z + dz) % NZ, ylo, yh, dz % NX, c))

    p_copy(1).start()
    for h in range(2):
        for dz in ORDER:
            for l in range(2):
                if dz == 0:
                    lt = (1 - ylo + l) % 2

                    @pl.when(x == 0)
                    def _():
                        pltpu.make_async_copy(asort.at[h, 0, lt], r1.at[0, 0, lt, h], rs1.at[0, 0, lt, h]).start()

                    @pl.when(x != 0)
                    def _():
                        a_copy(h, 0, l).start()
                else:
                    a_copy(h, dz, l).start()

    sort_p(XORDER[1])
    sort_p(XORDER[2])
    p_copy(2).start()
    sort_p(0)
    p_copy(3).start()
    own_p.start()

    flip = x // 3
    chunks = [(h, j, d, l) for h in range(2) for j in range(2) for d in (0, 1, 3, 2) for l in range(2)]

    def block(h, ys, xs, core, zi, ls):
        lane = pl.ds(pl.multiple_of((zi * 2 + ls) * BLK, BLK), BLK)
        return afin.at[h, ys * 8 + xs * 2 + core, :, lane]

    def y_copies(k):
        h, j, d, l = chunks[k]
        zi, xs, lt = (j + flip) % 2, (x + d) % NX, (1 - ylo + l) % 2
        src = r1.at[zi, xs, lt, h]
        dst = block(h, yh, xs, c, zi, ylo)
        rs = rsy.at[h, yh, xs, zi, ylo]
        out = [remote(src, dst, ssy.at[k, 0], rs, device(z, lt, 1 - yh, x, c))]
        if l == 0:
            out.append(remote(src, dst, ssy.at[k, 1], rs, device(z, lt, yh, x, c)))
        return src, rs1.at[zi, xs, lt, h], out, dst, rs

    def sources(k):
        h, j, d, l = chunks[k]
        zi, xs = (j + flip) % 2, (x + d) % NX
        ls = (ylo + 1 - l) % 2
        return [(h, (yh + dy) % 2, xs, zi, ls, dy) for dy in range(2)]

    def c_copies(k):
        return [remote(block(h, ys, xs, c, zi, ls), block(h, ys, xs, c, zi, ls), ssc.at[k, dy],
                       rsc.at[h, ys, xs, zi, ls], device(z, ylo, yh, x, 1 - c))
                for h, ys, xs, zi, ls, dy in sources(k)]

    lag = 6
    for k in range(len(chunks) + lag):
        if k < len(chunks):
            src, sem, out, dst, rs = y_copies(k)
            arrived(src, sem)
            for cp in out:
                cp.start()
            if chunks[k][3] == 1:
                pltpu.make_async_copy(src, dst, rs).start()
        if k >= lag:
            for (h, ys, xs, zi, ls, _), cp in zip(sources(k - lag), c_copies(k - lag)):
                arrived(block(h, ys, xs, c, zi, ls), rsy.at[h, ys, xs, zi, ls])
                cp.start()
    for k in range(len(chunks)):
        for h, ys, xs, zi, ls, _ in sources(k):
            arrived(block(h, ys, xs, 1 - c, zi, ls), rsc.at[h, ys, xs, zi, ls])

    blocks = ROWS // 32

    def part(i):
        return i // 2, (z // 4 + i % 2) % 2 * blocks

    def lhs(i):
        h, at = part(i)
        return afin[h, pl.ds(at, blocks)].reshape(ROWS, KLOC)

    def times(a, b):
        return lax.dot_general(a, b, (((1,), (1,)), ((), ())), preferred_element_type=jnp.float32)

    def x_copy(slot, i):
        d = XORDER[slot - 1]
        back = XORDER.index(NX - d)
        return remote(psend.at[slot - 1, i], rx.at[back, i], ssx.at[slot - 1, i],
                      rsx.at[back, i], device(z, ylo, yh, (x + d) % NX, c))

    arrived(pfin.at[0], rsp.at[0])
    arrived(pfin.at[1], rsp.at[1])
    for i in range(STEPS):
        v = times(lhs(i), pfin[0:2].reshape(256, KLOC))
        own[i] = v[:, :128]
        psend[0, i] = v[:, 128:].astype(psend.dtype)
        x_copy(1, i).start()
    for slot in (2, 3):
        arrived(pfin.at[slot], rsp.at[slot])
        for i in range(STEPS):
            psend[slot - 1, i] = times(lhs(i), pfin[slot]).astype(psend.dtype)
            x_copy(slot, i).start()

    def f_copy(i, j):
        h, at = part(i)
        to = at + j
        return remote(fsend.at[h, to], r2.at[h, space], ss2.at[i, j], rs2.at[h, space],
                      device(to // 2, to % 2, yh, x, c))

    for i in range(STEPS):
        h, at = part(i)
        total = own[i]
        for slot in range(3):
            arrived(rx.at[slot, i], rsx.at[slot, i])
            total = total + rx[slot, i].astype(jnp.float32)
        total = total.reshape(blocks, 32, 128)
        fsend[h, pl.ds(at, blocks)] = total.astype(fsend.dtype)
        tot[h, pl.ds(at, blocks)] = total
        for j in range(blocks):
            @pl.when(at + j != space)
            def _():
                f_copy(i, j).start()
    for h in range(2):
        acc = tot[h, space]
        for d in range(1, TILES):
            frm = (space + d) % TILES
            arrived(r2.at[h, frm], rs2.at[h, frm])
            acc = acc + r2[h, frm].astype(jnp.float32)
        o_ref[h * 32:(h + 1) * 32] = acc

    for h in range(2):
        for l in range(2):
            @pl.when(x != 0)
            def _():
                a_copy(h, 0, l).wait_send()
            for dz in range(1, NZ):
                a_copy(h, dz, l).wait_send()
    for slot in range(1, NX):
        p_copy(slot).wait_send()
        for i in range(STEPS):
            x_copy(slot, i).wait_send()
    for k in range(len(chunks)):
        for cp in y_copies(k)[2] + c_copies(k):
            cp.wait_send()
    for i in range(STEPS):
        for j in range(blocks):
            @pl.when(part(i)[1] + j != space)
            def _():
                f_copy(i, j).wait_send()


def exchange(idx_p, weights, a_sorted, primal):
    bf, f32 = jnp.bfloat16, jnp.float32
    dma = pltpu.SemaphoreType.DMA
    smem = pl.BlockSpec(memory_space=pltpu.SMEM)
    hbm = pl.BlockSpec(memory_space=pl.ANY)
    vmem = pl.BlockSpec(memory_space=pltpu.VMEM)
    return pl.pallas_call(
        main_kernel,
        in_specs=[smem, vmem, hbm, hbm],
        out_specs=vmem,
        out_shape=jax.ShapeDtypeStruct((64, 128), f32),
        scratch_shapes=[
            pltpu.VMEM((DEV_PEN, 128, PEN), bf),
            pltpu.VMEM((NX, 128, KLOC), bf),
            pltpu.VMEM((2, NX, 2, 2, 32, BLK), bf),
            pltpu.VMEM((2, 16, 32, KLOC), bf),
            pltpu.VMEM((NX, 128, KLOC), bf),
            pltpu.VMEM((STEPS, ROWS, 128), f32),
            pltpu.VMEM((3, STEPS, ROWS, 128), bf),
            pltpu.VMEM((3, STEPS, ROWS, 128), bf),
            pltpu.VMEM((2, TILES, 32, 128), f32),
            pltpu.VMEM((2, TILES, 32, 128), bf),
            pltpu.VMEM((2, TILES, 32, 128), bf),
            dma((1,)),
            dma((NZ, 2, 2)), dma((2, NX, 2, 2)),
            dma((3,)), dma((NX,)),
            dma((32, 2)), dma((2, 2, NX, 2, 2)),
            dma((32, 2)), dma((2, 2, NX, 2, 2)),
            dma((3, STEPS)), dma((3, STEPS)),
            dma((STEPS, ROWS // 32)), dma((2, TILES)),
        ],
        compiler_params=pltpu.CompilerParams(
            collective_id=0, has_side_effects=True, vmem_limit_bytes=60 * 1024 * 1024),
        name="exchange",
    )(idx_p.T, weights.reshape(DEV_PEN, 1, PEN), a_sorted, primal)


def on_device(primal, adjoint_pencils, weights, pencil_map):
    space = lax.axis_index("space")
    maps = pencil_map.reshape(TILES, DEV_PEN)
    target = maps // DEV_PEN
    before = jnp.arange(DEV_PEN)[None, :] < jnp.arange(DEV_PEN)[:, None]
    rank = jnp.sum((target[:, :, None] == target[:, None, :]) & before[None], axis=2, dtype=jnp.int32)
    of_rank = jnp.arange(SHARE, dtype=jnp.int32)[None, :, None]
    here = (target == space)[:, None, :] & (rank[:, None, :] == of_rank)
    idx_p = jnp.sum(jnp.where(here, maps[:, None, :] - space * DEV_PEN, 0), axis=2, dtype=jnp.int32)
    own_target = lax.dynamic_index_in_dim(target, space, 0, keepdims=True)
    own_rank = lax.dynamic_index_in_dim(rank, space, 0, keepdims=True)
    to = (own_target == jnp.arange(TILES, dtype=jnp.int32)[:, None])[:, None, :] & (own_rank[:, None, :] == of_rank)
    idx_a = jnp.sum(jnp.where(to, jnp.arange(DEV_PEN, dtype=jnp.int32), 0), axis=2, dtype=jnp.int32)
    return exchange(idx_p, weights, sort_adjoint(idx_a.T, adjoint_pencils), primal)


def solution(mesh):
    placed = (P("snap", "space"), P("snap", "space"), P("space"), P())
    return jax.shard_map(
        on_device, mesh=mesh, in_specs=placed, out_specs=P("space", "snap"), check_vma=False
    )
```

```python
import functools
import jax
import jax.numpy as jnp
from jax import lax
from jax.experimental import pallas as pl
from jax.experimental.pallas import tpu as pltpu
from jax.sharding import PartitionSpec as P

PEN = 128
NX, NZ = 4, 8
TILES = 16
DEV_PEN = 96
SHARE = 6
MESH = pl.DeviceIdType.MESH
BLK = SHARE * PEN
KLOC = 4 * BLK


def where_am_i():
    space = lax.axis_index("space")
    snap = lax.axis_index("snap")
    return space // 2, space % 2, snap // 8, (snap // 2) % NX, snap % 2


def device(z, ylo, yh, x, c):
    return {"space": z * 2 + ylo, "snap": yh * 8 + x * 2 + c}


ORDER = (0, 1, 7, 2, 6, 4, 3, 5)
XORDER = (1, 3, 2)
ROWS = 256
STEPS = 1024 // ROWS


def main_kernel(idx_a, idx_p, w_ref, a_hbm, p_hbm, o_ref, a_v, p_v, a3, p3, asort, psort, r1, afin, pfin,
                own, psend, rx, tot, r2,
                lsem, ss1, rs1, ssp, rsp, ssy, rsy, ssc, rsc, ssx, rsx, ss2, rs2):
    z, ylo, yh, x, c = where_am_i()
    space = z * 2 + ylo

    def remote(src, dst, ss, rs, dev):
        return pltpu.make_async_remote_copy(src_ref=src, dst_ref=dst, send_sem=ss, recv_sem=rs,
                                            device_id=dev, device_id_type=MESH)

    def arrived(ref, sem):
        pltpu.make_async_copy(ref, ref, sem).wait()

    load_a = pltpu.make_async_copy(a_hbm, a_v, lsem.at[0])
    load_p = pltpu.make_async_copy(p_hbm, p_v, lsem.at[1])
    load_a.start()
    load_p.start()

    bar = pltpu.get_barrier_semaphore()

    def greet(dev):
        pl.semaphore_signal(bar, inc=1, device_id=dev, device_id_type=MESH)

    for zi in range(2):
        for xs in range(NX):
            dev = device((z - x - 4 * zi + 2 * NZ) % NZ, ylo, yh, xs, c)
            if zi == 0 and xs == 0:
                @pl.when(x != 0)
                def _():
                    greet(dev)
            else:
                greet(dev)
    for d in range(1, NX):
        greet(device(z, ylo, yh, (x + d) % NX, c))
    greet(device(z, ylo, 1 - yh, x, c))
    greet(device(z, 1 - ylo, 0, x, c))
    greet(device(z, 1 - ylo, 1, x, c))
    greet(device(z, ylo, yh, x, 1 - c))
    for d in range(1, TILES):
        to = (space + d) % TILES
        greet(device(to // 2, to % 2, yh, x, c))

    load_a.wait()
    for i in range(DEV_PEN):
        a3[i] = a_v[:, i * PEN:(i + 1) * PEN]
    for dz in range(NZ):
        for lt in range(2):
            t = ((z + dz) % NZ) * 2 + lt
            for r in range(SHARE):
                v = a3[idx_a[r, t]]
                for h in range(2):
                    asort[dz, lt, h, :, r * PEN:(r + 1) * PEN] = v[h * 32:(h + 1) * 32]

    load_p.wait()
    for i in range(DEV_PEN):
        span = slice(i * PEN, (i + 1) * PEN)
        p3[i] = (p_v[:, span].astype(jnp.float32) * w_ref[:, span]).astype(jnp.bfloat16)

    pl.semaphore_wait(bar, 7 + 3 + 3 + 1 + 15 + (x + NX - 1) // NX)

    def a_copy(h, dz, l):
        lt = (1 - ylo + l) % 2
        return remote(asort.at[dz, lt, h], r1.at[dz // NX, x, lt, h], ss1.at[dz, l, h],
                      rs1.at[dz // NX, x, lt, h], device((z + dz) % NZ, ylo, yh, dz % NX, c))

    for h in range(2):
        for dz in ORDER:
            for l in range(2):
                if dz == 0:
                    lt = (1 - ylo + l) % 2

                    @pl.when(x == 0)
                    def _():
                        pltpu.make_async_copy(asort.at[0, lt, h], r1.at[0, 0, lt, h], rs1.at[0, 0, lt, h]).start()

                    @pl.when(x != 0)
                    def _():
                        a_copy(h, 0, l).start()
                else:
                    a_copy(h, dz, l).start()

    def p_copy(slot):
        d = XORDER[slot - 1]
        return remote(psort.at[d], pfin.at[XORDER.index(NX - d) + 1], ssp.at[slot - 1],
                      rsp.at[XORDER.index(NX - d) + 1], device(z, ylo, yh, (x + d) % NX, c))

    own_p = pltpu.make_async_copy(psort.at[0], pfin.at[0], rsp.at[0])
    for step, d in enumerate(XORDER + (0,)):
        for zi in range(2):
            dz = (x + d) % NX + NX * zi
            for ls in range(2):
                src = ((z - dz + NZ) % NZ) * 2 + ls
                for r in range(SHARE):
                    i = idx_p[r, src]
                    at = ((zi * 2 + ls) * SHARE + r) * PEN
                    psort[d, :, at:at + PEN] = p3[i]
        if step >= 1:
            p_copy(step).start()
    own_p.start()

    flip = x // 3
    chunks = [(h, j, d, l) for h in range(2) for j in range(2) for d in (0, 1, 3, 2) for l in range(2)]

    def block(h, ys, xs, core, zi, ls):
        lane = pl.ds(pl.multiple_of((zi * 2 + ls) * BLK, BLK), BLK)
        return afin.at[h, ys * 8 + xs * 2 + core, :, lane]

    def y_copies(k):
        h, j, d, l = chunks[k]
        zi, xs, lt = (j + flip) % 2, (x + d) % NX, (1 - ylo + l) % 2
        src = r1.at[zi, xs, lt, h]
        dst = block(h, yh, xs, c, zi, ylo)
        rs = rsy.at[h, yh, xs, zi, ylo]
        out = [remote(src, dst, ssy.at[k, 0], rs, device(z, lt, 1 - yh, x, c))]
        if l == 0:
            out.append(remote(src, dst, ssy.at[k, 1], rs, device(z, lt, yh, x, c)))
        return src, rs1.at[zi, xs, lt, h], out, dst, rs

    def sources(k):
        h, j, d, l = chunks[k]
        zi, xs = (j + flip) % 2, (x + d) % NX
        ls = (ylo + 1 - l) % 2
        return [(h, (yh + dy) % 2, xs, zi, ls, dy) for dy in range(2)]

    def c_copies(k):
        return [remote(block(h, ys, xs, c, zi, ls), block(h, ys, xs, c, zi, ls), ssc.at[k, dy],
                       rsc.at[h, ys, xs, zi, ls], device(z, ylo, yh, x, 1 - c))
                for h, ys, xs, zi, ls, dy in sources(k)]

    lag = 6
    for k in range(len(chunks) + lag):
        if k < len(chunks):
            src, sem, out, dst, rs = y_copies(k)
            arrived(src, sem)
            for cp in out:
                cp.start()
            if chunks[k][3] == 1:
                pltpu.make_async_copy(src, dst, rs).start()
        if k >= lag:
            for (h, ys, xs, zi, ls, _), cp in zip(sources(k - lag), c_copies(k - lag)):
                arrived(block(h, ys, xs, c, zi, ls), rsy.at[h, ys, xs, zi, ls])
                cp.start()
    for k in range(len(chunks)):
        for h, ys, xs, zi, ls, _ in sources(k):
            arrived(block(h, ys, xs, 1 - c, zi, ls), rsc.at[h, ys, xs, zi, ls])

    blocks = ROWS // 32

    def part(i):
        return i // 2, (z // 4 + i % 2) % 2 * blocks

    def lhs(i):
        h, at = part(i)
        return afin[h, pl.ds(at, blocks)].reshape(ROWS, KLOC)

    def times(a, b):
        return lax.dot_general(a, b, (((1,), (1,)), ((), ())), preferred_element_type=jnp.float32)

    def x_copy(slot, i):
        d = XORDER[slot - 1]
        back = XORDER.index(NX - d)
        return remote(psend.at[slot - 1, i], rx.at[back, i], ssx.at[slot - 1, i],
                      rsx.at[back, i], device(z, ylo, yh, (x + d) % NX, c))

    arrived(pfin.at[0], rsp.at[0])
    arrived(pfin.at[1], rsp.at[1])
    for i in range(STEPS):
        v = times(lhs(i), pfin[0:2].reshape(256, KLOC))
        own[i] = v[:, :128]
        psend[0, i] = v[:, 128:].astype(psend.dtype)
        x_copy(1, i).start()
    for slot in (2, 3):
        arrived(pfin.at[slot], rsp.at[slot])
        for i in range(STEPS):
            psend[slot - 1, i] = times(lhs(i), pfin[slot]).astype(psend.dtype)
            x_copy(slot, i).start()

    def f_copy(i, j):
        h, at = part(i)
        to = at + j
        return remote(tot.at[h, to], r2.at[h, space], ss2.at[i, j], rs2.at[h, space],
                      device(to // 2, to % 2, yh, x, c))

    for i in range(STEPS):
        h, at = part(i)
        total = own[i]
        for slot in range(3):
            arrived(rx.at[slot, i], rsx.at[slot, i])
            total = total + rx[slot, i].astype(jnp.float32)
        tot[h, pl.ds(at, blocks)] = total.reshape(blocks, 32, 128)
        for j in range(blocks):
            @pl.when(at + j != space)
            def _():
                f_copy(i, j).start()
    for h in range(2):
        acc = tot[h, space]
        for d in range(1, TILES):
            frm = (space + d) % TILES
            arrived(r2.at[h, frm], rs2.at[h, frm])
            acc = acc + r2[h, frm]
        o_ref[h * 32:(h + 1) * 32] = acc

    for h in range(2):
        for l in range(2):
            @pl.when(x != 0)
            def _():
                a_copy(h, 0, l).wait_send()
            for dz in range(1, NZ):
                a_copy(h, dz, l).wait_send()
    for slot in range(1, NX):
        p_copy(slot).wait_send()
        for i in range(STEPS):
            x_copy(slot, i).wait_send()
    for k in range(len(chunks)):
        for cp in y_copies(k)[2] + c_copies(k):
            cp.wait_send()
    for i in range(STEPS):
        for j in range(blocks):
            @pl.when(part(i)[1] + j != space)
            def _():
                f_copy(i, j).wait_send()


def exchange(idx_a, idx_p, weights, adjoint, primal):
    bf, f32 = jnp.bfloat16, jnp.float32
    dma = pltpu.SemaphoreType.DMA
    smem = pl.BlockSpec(memory_space=pltpu.SMEM)
    hbm = pl.BlockSpec(memory_space=pl.ANY)
    vmem = pl.BlockSpec(memory_space=pltpu.VMEM)
    return pl.pallas_call(
        main_kernel,
        in_specs=[smem, smem, vmem, hbm, hbm],
        out_specs=vmem,
        out_shape=jax.ShapeDtypeStruct((64, 128), f32),
        scratch_shapes=[
            pltpu.VMEM(adjoint.shape, bf),
            pltpu.VMEM(primal.shape, bf),
            pltpu.VMEM((DEV_PEN, 64, PEN), bf),
            pltpu.VMEM((DEV_PEN, 128, PEN), bf),
            pltpu.VMEM((NZ, 2, 2, 32, BLK), bf),
            pltpu.VMEM((NX, 128, KLOC), bf),
            pltpu.VMEM((2, NX, 2, 2, 32, BLK), bf),
            pltpu.VMEM((2, 16, 32, KLOC), bf),
            pltpu.VMEM((NX, 128, KLOC), bf),
            pltpu.VMEM((STEPS, ROWS, 128), f32),
            pltpu.VMEM((3, STEPS, ROWS, 128), bf),
            pltpu.VMEM((3, STEPS, ROWS, 128), bf),
            pltpu.VMEM((2, TILES, 32, 128), f32),
            pltpu.VMEM((2, TILES, 32, 128), f32),
            dma((2,)),
            dma((NZ, 2, 2)), dma((2, NX, 2, 2)),
            dma((3,)), dma((NX,)),
            dma((32, 2)), dma((2, 2, NX, 2, 2)),
            dma((32, 2)), dma((2, 2, NX, 2, 2)),
            dma((3, STEPS)), dma((3, STEPS)),
            dma((STEPS, ROWS // 32)), dma((2, TILES)),
        ],
        compiler_params=pltpu.CompilerParams(
            collective_id=0, has_side_effects=True, vmem_limit_bytes=60 * 1024 * 1024),
        name="exchange",
    )(idx_a.T, idx_p.T, weights[None], adjoint, primal)


def on_device(primal, adjoint_pencils, weights, pencil_map):
    space = lax.axis_index("space")
    maps = pencil_map.reshape(TILES, DEV_PEN)
    target = maps // DEV_PEN
    before = jnp.arange(DEV_PEN)[None, :] < jnp.arange(DEV_PEN)[:, None]
    rank = jnp.sum((target[:, :, None] == target[:, None, :]) & before[None], axis=2, dtype=jnp.int32)
    of_rank = jnp.arange(SHARE, dtype=jnp.int32)[None, :, None]
    here = (target == space)[:, None, :] & (rank[:, None, :] == of_rank)
    idx_p = jnp.sum(jnp.where(here, maps[:, None, :] - space * DEV_PEN, 0), axis=2, dtype=jnp.int32)
    own_target = lax.dynamic_index_in_dim(target, space, 0, keepdims=True)
    own_rank = lax.dynamic_index_in_dim(rank, space, 0, keepdims=True)
    to = (own_target == jnp.arange(TILES, dtype=jnp.int32)[:, None])[:, None, :] & (own_rank[:, None, :] == of_rank)
    idx_a = jnp.sum(jnp.where(to, jnp.arange(DEV_PEN, dtype=jnp.int32), 0), axis=2, dtype=jnp.int32)
    return exchange(idx_a, idx_p, weights, adjoint_pencils, primal)


def solution(mesh):
    placed = (P("snap", "space"), P("snap", "space"), P("space"), P())
    return jax.shard_map(
        on_device, mesh=mesh, in_specs=placed, out_specs=P("space", "snap"), check_vma=False
    )
```

```python
import functools
import jax
import jax.numpy as jnp
from jax import lax
from jax.experimental import pallas as pl
from jax.experimental.pallas import tpu as pltpu
from jax.sharding import PartitionSpec as P

PEN = 128
NX, NZ = 4, 8
TILES = 16
DEV_PEN = 96
SHARE = 6
MESH = pl.DeviceIdType.MESH
BLK = SHARE * PEN
KLOC = 4 * BLK


def where_am_i():
    space = lax.axis_index("space")
    snap = lax.axis_index("snap")
    return space // 2, space % 2, snap // 8, (snap // 2) % NX, snap % 2


def device(z, ylo, yh, x, c):
    return {"space": z * 2 + ylo, "snap": yh * 8 + x * 2 + c}


ORDER = (0, 1, 7, 2, 6, 4, 3, 5)
XORDER = (1, 3, 2)
ROWS = 256


def main_kernel(idx_a, idx_p, w_ref, a_hbm, p_hbm, o_ref, a_v, p_v, a3, p3, asort, psort, r1, afin, pfin,
                keep, ysend, yrecv, zsum, zsend, zrecv, xsend, xrecv,
                lsem, ss1, rs1, ssp, rsp, ssy, rsy, ssc, rsc, ssf, rsf, ssz, rsz, ssx, rsx):
    z, ylo, yh, x, c = where_am_i()

    def remote(src, dst, ss, rs, dev):
        return pltpu.make_async_remote_copy(src_ref=src, dst_ref=dst, send_sem=ss, recv_sem=rs,
                                            device_id=dev, device_id_type=MESH)

    def arrived(ref, sem):
        pltpu.make_async_copy(ref, ref, sem).wait()

    load_a = pltpu.make_async_copy(a_hbm, a_v, lsem.at[0])
    load_p = pltpu.make_async_copy(p_hbm, p_v, lsem.at[1])
    load_a.start()
    load_p.start()

    bar = pltpu.get_barrier_semaphore()

    def greet(dev):
        pl.semaphore_signal(bar, inc=1, device_id=dev, device_id_type=MESH)

    for zi in range(2):
        for xs in range(NX):
            dev = device((z - x - 4 * zi + 2 * NZ) % NZ, ylo, yh, xs, c)
            if zi == 0 and xs == 0:
                @pl.when(x != 0)
                def _():
                    greet(dev)
            else:
                greet(dev)
    for d in range(1, NX):
        greet(device(z, ylo, yh, (x + d) % NX, c))
    greet(device(z, ylo, 1 - yh, x, c))
    greet(device(z, 1 - ylo, 0, x, c))
    greet(device(z, 1 - ylo, 1, x, c))
    greet(device(z, ylo, yh, x, 1 - c))
    for d in range(1, NZ):
        greet(device((z + d) % NZ, ylo, yh, x, c))

    load_a.wait()
    for i in range(DEV_PEN):
        a3[i] = a_v[:, i * PEN:(i + 1) * PEN]
    for dz in range(NZ):
        for lt in range(2):
            t = ((z + dz) % NZ) * 2 + lt
            for r in range(SHARE):
                v = a3[idx_a[r, t]]
                for h in range(2):
                    asort[dz, lt, h, :, r * PEN:(r + 1) * PEN] = v[h * 32:(h + 1) * 32]

    load_p.wait()
    for i in range(DEV_PEN):
        span = slice(i * PEN, (i + 1) * PEN)
        p3[i] = (p_v[:, span].astype(jnp.float32) * w_ref[:, span]).astype(jnp.bfloat16)

    pl.semaphore_wait(bar, 7 + 3 + 3 + 1 + 7 + (x + NX - 1) // NX)

    def a_copy(h, dz, l):
        lt = (1 - ylo + l) % 2
        return remote(asort.at[dz, lt, h], r1.at[dz // NX, x, lt, h], ss1.at[dz, l, h],
                      rs1.at[dz // NX, x, lt, h], device((z + dz) % NZ, ylo, yh, dz % NX, c))

    for h in range(2):
        for dz in ORDER:
            for l in range(2):
                if dz == 0:
                    lt = (1 - ylo + l) % 2

                    @pl.when(x == 0)
                    def _():
                        pltpu.make_async_copy(asort.at[0, lt, h], r1.at[0, 0, lt, h], rs1.at[0, 0, lt, h]).start()

                    @pl.when(x != 0)
                    def _():
                        a_copy(h, 0, l).start()
                else:
                    a_copy(h, dz, l).start()

    def p_copy(slot):
        d = XORDER[slot - 1]
        return remote(psort.at[d], pfin.at[XORDER.index(NX - d) + 1], ssp.at[slot - 1],
                      rsp.at[XORDER.index(NX - d) + 1], device(z, ylo, yh, (x + d) % NX, c))

    own_p = pltpu.make_async_copy(psort.at[0], pfin.at[0], rsp.at[0])
    for step, d in enumerate(XORDER + (0,)):
        for zi in range(2):
            dz = (x + d) % NX + NX * zi
            for ls in range(2):
                src = ((z - dz + NZ) % NZ) * 2 + ls
                for r in range(SHARE):
                    i = idx_p[r, src]
                    at = ((zi * 2 + ls) * SHARE + r) * PEN
                    psort[d, :, at:at + PEN] = p3[i]
        if step >= 1:
            p_copy(step).start()
    own_p.start()

    flip = x // 3
    chunks = [(h, j, d, l) for h in range(2) for j in range(2) for d in (0, 1, 3, 2) for l in range(2)]

    def block(h, ys, xs, core, zi, ls):
        lane = pl.ds(pl.multiple_of((zi * 2 + ls) * BLK, BLK), BLK)
        return afin.at[h, core * NZ + ys * NX + xs, :, lane]

    def y_copies(k):
        h, j, d, l = chunks[k]
        zi, xs, lt = (j + flip) % 2, (x + d) % NX, (1 - ylo + l) % 2
        src = r1.at[zi, xs, lt, h]
        dst = block(h, yh, xs, c, zi, ylo)
        rs = rsy.at[h, yh, xs, zi, ylo]
        out = [remote(src, dst, ssy.at[k, 0], rs, device(z, lt, 1 - yh, x, c))]
        if l == 0:
            out.append(remote(src, dst, ssy.at[k, 1], rs, device(z, lt, yh, x, c)))
        return src, rs1.at[zi, xs, lt, h], out, dst, rs

    def sources(k):
        h, j, d, l = chunks[k]
        zi, xs = (j + flip) % 2, (x + d) % NX
        ls = (ylo + 1 - l) % 2
        return [(h, (yh + dy) % 2, xs, zi, ls, dy) for dy in range(2)]

    def c_copies(k):
        return [remote(block(h, ys, xs, c, zi, ls), block(h, ys, xs, c, zi, ls), ssc.at[k, dy],
                       rsc.at[h, ys, xs, zi, ls], device(z, ylo, yh, x, 1 - c))
                for h, ys, xs, zi, ls, dy in sources(k)]

    lag = 6
    for k in range(len(chunks) + lag):
        if k < len(chunks):
            src, sem, out, dst, rs = y_copies(k)
            arrived(src, sem)
            for cp in out:
                cp.start()
            if chunks[k][3] == 1:
                pltpu.make_async_copy(src, dst, rs).start()
        if k >= lag:
            for (h, ys, xs, zi, ls, _), cp in zip(sources(k - lag), c_copies(k - lag)):
                arrived(block(h, ys, xs, c, zi, ls), rsy.at[h, ys, xs, zi, ls])
                cp.start()
    for k in range(len(chunks)):
        for h, ys, xs, zi, ls, _ in sources(k):
            arrived(block(h, ys, xs, 1 - c, zi, ls), rsc.at[h, ys, xs, zi, ls])

    def lhs(h, l):
        at = pl.multiple_of((ylo + 1 - l) % 2 * NZ, NZ)
        return afin[h, pl.ds(at, NZ)].reshape(ROWS, KLOC)

    def times(a, b):
        return lax.dot_general(a, b, (((1,), (1,)), ((), ())), preferred_element_type=jnp.float32)

    def over_y(slot, h):
        return remote(ysend.at[slot, h], yrecv.at[slot, h], ssf.at[slot, h], rsf.at[slot, h],
                      device(z, 1 - ylo, yh, x, c))

    def over_z(slot, d):
        to = (z + d) % NZ
        return remote(zsend.at[slot, to], zrecv.at[slot, z], ssz.at[slot, d - 1], rsz.at[slot, z],
                      device(to, ylo, yh, x, c))

    def over_x(slot):
        d = XORDER[slot - 1]
        back = XORDER.index(NX - d)
        return remote(xsend.at[slot - 1], xrecv.at[back], ssx.at[slot - 1], rsx.at[back],
                      device(z, ylo, yh, (x + d) % NX, c))

    def to_z(slot):
        for h in range(2):
            arrived(yrecv.at[slot, h], rsf.at[slot, h])
            v = (keep[slot, h] + yrecv[slot, h].astype(jnp.float32)).reshape(NZ, 32, 128)
            zsum[slot, :, h] = v
            zsend[slot, :, h] = v.astype(zsend.dtype)
        for d in (4, 3, 5, 2, 6, 1, 7):
            over_z(slot, d).start()

    def summed(slot):
        acc = zsum[slot, z]
        for d in (1, 7, 2, 6, 3, 5, 4):
            frm = (z + d) % NZ
            arrived(zrecv.at[slot, frm], rsz.at[slot, frm])
            acc = acc + zrecv[slot, frm].astype(jnp.float32)
        return acc

    arrived(pfin.at[0], rsp.at[0])
    arrived(pfin.at[1], rsp.at[1])
    for l in range(2):
        for h in range(2):
            v = times(lhs(h, l), pfin[0:2].reshape(256, KLOC))
            for slot in range(2):
                w = v[:, slot * 128:(slot + 1) * 128]
                if l == 0:
                    ysend[slot, h] = w.astype(ysend.dtype)
                    over_y(slot, h).start()
                else:
                    keep[slot, h] = w

    def one(slot):
        arrived(pfin.at[slot], rsp.at[slot])
        for l in range(2):
            for h in range(2):
                w = times(lhs(h, l), pfin[slot])
                if l == 0:
                    ysend[slot, h] = w.astype(ysend.dtype)
                    over_y(slot, h).start()
                else:
                    keep[slot, h] = w

    one(2)
    for slot in (1, 0, 2):
        to_z(slot)
    one(3)
    to_z(3)
    for slot in (1, 2):
        xsend[slot - 1] = summed(slot)
        over_x(slot).start()
    acc = summed(0)
    xsend[2] = summed(3)
    over_x(3).start()
    for slot in range(3):
        arrived(xrecv.at[slot], rsx.at[slot])
        acc = acc + xrecv[slot]
    o_ref[...] = acc.reshape(64, 128)

    for h in range(2):
        for l in range(2):
            @pl.when(x != 0)
            def _():
                a_copy(h, 0, l).wait_send()
            for dz in range(1, NZ):
                a_copy(h, dz, l).wait_send()
    for slot in range(1, NX):
        p_copy(slot).wait_send()
        over_x(slot).wait_send()
    for k in range(len(chunks)):
        for cp in y_copies(k)[2] + c_copies(k):
            cp.wait_send()
    for slot in range(NX):
        for h in range(2):
            over_y(slot, h).wait_send()
        for d in range(1, NZ):
            over_z(slot, d).wait_send()


def exchange(idx_a, idx_p, weights, adjoint, primal):
    bf, f32 = jnp.bfloat16, jnp.float32
    dma = pltpu.SemaphoreType.DMA
    smem = pl.BlockSpec(memory_space=pltpu.SMEM)
    hbm = pl.BlockSpec(memory_space=pl.ANY)
    vmem = pl.BlockSpec(memory_space=pltpu.VMEM)
    return pl.pallas_call(
        main_kernel,
        in_specs=[smem, smem, vmem, hbm, hbm],
        out_specs=vmem,
        out_shape=jax.ShapeDtypeStruct((64, 128), f32),
        scratch_shapes=[
            pltpu.VMEM(adjoint.shape, bf),
            pltpu.VMEM(primal.shape, bf),
            pltpu.VMEM((DEV_PEN, 64, PEN), bf),
            pltpu.VMEM((DEV_PEN, 128, PEN), bf),
            pltpu.VMEM((NZ, 2, 2, 32, BLK), bf),
            pltpu.VMEM((NX, 128, KLOC), bf),
            pltpu.VMEM((2, NX, 2, 2, 32, BLK), bf),
            pltpu.VMEM((2, 16, 32, KLOC), bf),
            pltpu.VMEM((NX, 128, KLOC), bf),
            pltpu.VMEM((NX, 2, ROWS, 128), f32),
            pltpu.VMEM((NX, 2, ROWS, 128), bf),
            pltpu.VMEM((NX, 2, ROWS, 128), bf),
            pltpu.VMEM((NX, NZ, 2, 32, 128), f32),
            pltpu.VMEM((NX, NZ, 2, 32, 128), bf),
            pltpu.VMEM((NX, NZ, 2, 32, 128), bf),
            pltpu.VMEM((3, 2, 32, 128), f32),
            pltpu.VMEM((3, 2, 32, 128), f32),
            dma((2,)),
            dma((NZ, 2, 2)), dma((2, NX, 2, 2)),
            dma((3,)), dma((NX,)),
            dma((32, 2)), dma((2, 2, NX, 2, 2)),
            dma((32, 2)), dma((2, 2, NX, 2, 2)),
            dma((NX, 2)), dma((NX, 2)),
            dma((NX, NZ - 1)), dma((NX, NZ)),
            dma((3,)), dma((3,)),
        ],
        compiler_params=pltpu.CompilerParams(
            collective_id=0, has_side_effects=True, vmem_limit_bytes=60 * 1024 * 1024),
        name="exchange",
    )(idx_a.T, idx_p.T, weights[None], adjoint, primal)


def on_device(primal, adjoint_pencils, weights, pencil_map):
    space = lax.axis_index("space")
    maps = pencil_map.reshape(TILES, DEV_PEN)
    target = maps // DEV_PEN
    before = jnp.arange(DEV_PEN)[None, :] < jnp.arange(DEV_PEN)[:, None]
    rank = jnp.sum((target[:, :, None] == target[:, None, :]) & before[None], axis=2, dtype=jnp.int32)
    of_rank = jnp.arange(SHARE, dtype=jnp.int32)[None, :, None]
    here = (target == space)[:, None, :] & (rank[:, None, :] == of_rank)
    idx_p = jnp.sum(jnp.where(here, maps[:, None, :] - space * DEV_PEN, 0), axis=2, dtype=jnp.int32)
    own_target = lax.dynamic_index_in_dim(target, space, 0, keepdims=True)
    own_rank = lax.dynamic_index_in_dim(rank, space, 0, keepdims=True)
    to = (own_target == jnp.arange(TILES, dtype=jnp.int32)[:, None])[:, None, :] & (own_rank[:, None, :] == of_rank)
    idx_a = jnp.sum(jnp.where(to, jnp.arange(DEV_PEN, dtype=jnp.int32), 0), axis=2, dtype=jnp.int32)
    return exchange(idx_a, idx_p, weights, adjoint_pencils, primal)


def solution(mesh):
    placed = (P("snap", "space"), P("snap", "space"), P("space"), P())
    return jax.shard_map(
        on_device, mesh=mesh, in_specs=placed, out_specs=P("space", "snap"), check_vma=False
    )
```

```python
import functools
import jax
import jax.numpy as jnp
from jax import lax
from jax.experimental import pallas as pl
from jax.experimental.pallas import tpu as pltpu
from jax.sharding import PartitionSpec as P

PEN = 128
NX, NZ = 4, 8
TILES = 16
DEV_PEN = 96
SHARE = 6
MESH = pl.DeviceIdType.MESH
BLK = SHARE * PEN
KLOC = 4 * BLK


def where_am_i():
    space = lax.axis_index("space")
    snap = lax.axis_index("snap")
    return space // 2, space % 2, snap // 8, (snap // 2) % NX, snap % 2


def device(z, ylo, yh, x, c):
    return {"space": z * 2 + ylo, "snap": yh * 8 + x * 2 + c}


ORDER = (0, 1, 7, 2, 6, 4, 3, 5)
XORDER = (1, 3, 2)
ROWS = 256


def main_kernel(idx_a, idx_p, w_ref, a_hbm, p_hbm, o_ref, a_v, p_v, a3, p3, asort, psort, r1, afin, pfin,
                keep, ysend, yrecv, zsum, zsend, zrecv, xsend, xrecv,
                lsem, ss1, rs1, ssp, rsp, ssy, rsy, ssc, rsc, ssf, rsf, ssz, rsz, ssx, rsx):
    z, ylo, yh, x, c = where_am_i()

    def remote(src, dst, ss, rs, dev):
        return pltpu.make_async_remote_copy(src_ref=src, dst_ref=dst, send_sem=ss, recv_sem=rs,
                                            device_id=dev, device_id_type=MESH)

    def arrived(ref, sem):
        pltpu.make_async_copy(ref, ref, sem).wait()

    load_a = pltpu.make_async_copy(a_hbm, a_v, lsem.at[0])
    load_p = pltpu.make_async_copy(p_hbm, p_v, lsem.at[1])
    load_a.start()
    load_p.start()

    bar = pltpu.get_barrier_semaphore()

    def greet(dev):
        pl.semaphore_signal(bar, inc=1, device_id=dev, device_id_type=MESH)

    for zi in range(2):
        for xs in range(NX):
            dev = device((z - x - 4 * zi + 2 * NZ) % NZ, ylo, yh, xs, c)
            if zi == 0 and xs == 0:
                @pl.when(x != 0)
                def _():
                    greet(dev)
            else:
                greet(dev)
    for d in range(1, NX):
        greet(device(z, ylo, yh, (x + d) % NX, c))
    greet(device(z, ylo, 1 - yh, x, c))
    greet(device(z, 1 - ylo, 0, x, c))
    greet(device(z, 1 - ylo, 1, x, c))
    greet(device(z, ylo, yh, x, 1 - c))
    for d in range(1, NZ):
        greet(device((z + d) % NZ, ylo, yh, x, c))

    load_a.wait()
    for i in range(DEV_PEN):
        a3[i] = a_v[:, i * PEN:(i + 1) * PEN]
    for dz in range(NZ):
        for lt in range(2):
            t = ((z + dz) % NZ) * 2 + lt
            for r in range(SHARE):
                v = a3[idx_a[r, t]]
                for h in range(2):
                    asort[dz, lt, h, :, r * PEN:(r + 1) * PEN] = v[h * 32:(h + 1) * 32]

    load_p.wait()
    for i in range(DEV_PEN):
        span = slice(i * PEN, (i + 1) * PEN)
        p3[i] = (p_v[:, span].astype(jnp.float32) * w_ref[:, span]).astype(jnp.bfloat16)

    pl.semaphore_wait(bar, 7 + 3 + 3 + 1 + 7 + (x + NX - 1) // NX)

    def a_copy(h, dz, l):
        lt = (1 - ylo + l) % 2
        return remote(asort.at[dz, lt, h], r1.at[dz // NX, x, lt, h], ss1.at[dz, l, h],
                      rs1.at[dz // NX, x, lt, h], device((z + dz) % NZ, ylo, yh, dz % NX, c))

    for h in range(2):
        for dz in ORDER:
            for l in range(2):
                if dz == 0:
                    lt = (1 - ylo + l) % 2

                    @pl.when(x == 0)
                    def _():
                        pltpu.make_async_copy(asort.at[0, lt, h], r1.at[0, 0, lt, h], rs1.at[0, 0, lt, h]).start()

                    @pl.when(x != 0)
                    def _():
                        a_copy(h, 0, l).start()
                else:
                    a_copy(h, dz, l).start()

    def p_copy(slot):
        d = XORDER[slot - 1]
        return remote(psort.at[d], pfin.at[XORDER.index(NX - d) + 1], ssp.at[slot - 1],
                      rsp.at[XORDER.index(NX - d) + 1], device(z, ylo, yh, (x + d) % NX, c))

    own_p = pltpu.make_async_copy(psort.at[0], pfin.at[0], rsp.at[0])
    for step, d in enumerate(XORDER + (0,)):
        for zi in range(2):
            dz = (x + d) % NX + NX * zi
            for ls in range(2):
                src = ((z - dz + NZ) % NZ) * 2 + ls
                for r in range(SHARE):
                    i = idx_p[r, src]
                    at = ((zi * 2 + ls) * SHARE + r) * PEN
                    psort[d, :, at:at + PEN] = p3[i]
        if step >= 1:
            p_copy(step).start()
    own_p.start()

    flip = x // 3
    chunks = [(h, j, d, l) for h in range(2) for j in range(2) for d in (0, 1, 3, 2) for l in range(2)]

    def block(h, ys, xs, core, zi, ls):
        lane = pl.ds(pl.multiple_of((zi * 2 + ls) * BLK, BLK), BLK)
        return afin.at[h, core * NZ + ys * NX + xs, :, lane]

    def y_copies(k):
        h, j, d, l = chunks[k]
        zi, xs, lt = (j + flip) % 2, (x + d) % NX, (1 - ylo + l) % 2
        src = r1.at[zi, xs, lt, h]
        dst = block(h, yh, xs, c, zi, ylo)
        rs = rsy.at[h, yh, xs, zi, ylo]
        out = [remote(src, dst, ssy.at[k, 0], rs, device(z, lt, 1 - yh, x, c))]
        if l == 0:
            out.append(remote(src, dst, ssy.at[k, 1], rs, device(z, lt, yh, x, c)))
        return src, rs1.at[zi, xs, lt, h], out, dst, rs

    def sources(k):
        h, j, d, l = chunks[k]
        zi, xs = (j + flip) % 2, (x + d) % NX
        ls = (ylo + 1 - l) % 2
        return [(h, (yh + dy) % 2, xs, zi, ls, dy) for dy in range(2)]

    def c_copies(k):
        return [remote(block(h, ys, xs, c, zi, ls), block(h, ys, xs, c, zi, ls), ssc.at[k, dy],
                       rsc.at[h, ys, xs, zi, ls], device(z, ylo, yh, x, 1 - c))
                for h, ys, xs, zi, ls, dy in sources(k)]

    def lhs(h, l):
        at = pl.multiple_of((ylo + 1 - l) % 2 * NZ, NZ)
        return afin[h, pl.ds(at, NZ)].reshape(ROWS, KLOC)

    def times(a, b):
        return lax.dot_general(a, b, (((1,), (1,)), ((), ())), preferred_element_type=jnp.float32)

    def over_y(slot, h):
        return remote(ysend.at[slot, h], yrecv.at[slot, h], ssf.at[slot, h], rsf.at[slot, h],
                      device(z, 1 - ylo, yh, x, c))

    def give(slot, h, l, w):
        if l == 0:
            ysend[slot, h] = w.astype(ysend.dtype)
            over_y(slot, h).start()
        else:
            keep[slot, h] = w

    def single(slot, h, l):
        give(slot, h, l, times(lhs(h, l), pfin[slot]))

    def pair(h):
        for l in range(2):
            v = times(lhs(h, l), pfin[0:2].reshape(256, KLOC))
            for slot in range(2):
                give(slot, h, l, v[:, slot * 128:(slot + 1) * 128])

    def one(slot, h):
        for l in range(2):
            single(slot, h, l)

    def from_core(k):
        for h, ys, xs, zi, ls, _ in sources(k):
            arrived(block(h, ys, xs, 1 - c, zi, ls), rsc.at[h, ys, xs, zi, ls])

    lag = 6
    for k in range(len(chunks) + lag):
        if k < len(chunks):
            src, sem, out, dst, rs = y_copies(k)
            arrived(src, sem)
            for cp in out:
                cp.start()
            if chunks[k][3] == 1:
                pltpu.make_async_copy(src, dst, rs).start()
        if k >= lag:
            for (h, ys, xs, zi, ls, _), cp in zip(sources(k - lag), c_copies(k - lag)):
                arrived(block(h, ys, xs, c, zi, ls), rsy.at[h, ys, xs, zi, ls])
                cp.start()
        if k == 27:
            for m in range(len(chunks) // 2):
                from_core(m)
            arrived(pfin.at[0], rsp.at[0])
            arrived(pfin.at[1], rsp.at[1])
            pair(0)
        if k == 31:
            arrived(pfin.at[2], rsp.at[2])
            one(2, 0)

    def over_z(slot, d):
        to = (z + d) % NZ
        return remote(zsend.at[slot, to], zrecv.at[slot, z], ssz.at[slot, d - 1], rsz.at[slot, z],
                      device(to, ylo, yh, x, c))

    def over_x(slot):
        d = XORDER[slot - 1]
        back = XORDER.index(NX - d)
        return remote(xsend.at[slot - 1], xrecv.at[back], ssx.at[slot - 1], rsx.at[back],
                      device(z, ylo, yh, (x + d) % NX, c))

    def to_z(slot):
        for h in range(2):
            arrived(yrecv.at[slot, h], rsf.at[slot, h])
            v = (keep[slot, h] + yrecv[slot, h].astype(jnp.float32)).reshape(NZ, 32, 128)
            zsum[slot, :, h] = v
            zsend[slot, :, h] = v.astype(zsend.dtype)
        for d in (4, 3, 5, 2, 6, 1, 7):
            over_z(slot, d).start()

    def summed(slot):
        acc = zsum[slot, z]
        for d in (1, 7, 2, 6, 3, 5, 4):
            frm = (z + d) % NZ
            arrived(zrecv.at[slot, frm], rsz.at[slot, frm])
            acc = acc + zrecv[slot, frm].astype(jnp.float32)
        return acc

    for k in range(len(chunks) // 2, len(chunks)):
        from_core(k)
    pair(1)
    one(2, 1)
    for slot in (1, 0):
        to_z(slot)
    arrived(pfin.at[3], rsp.at[3])
    for l in range(2):
        for h in range(2):
            single(3, h, l)
    for slot in (2, 3):
        to_z(slot)
    for slot in (1, 2):
        xsend[slot - 1] = summed(slot)
        over_x(slot).start()
    acc = summed(0)
    xsend[2] = summed(3)
    over_x(3).start()
    for slot in range(3):
        arrived(xrecv.at[slot], rsx.at[slot])
        acc = acc + xrecv[slot]
    o_ref[...] = acc.reshape(64, 128)

    for h in range(2):
        for l in range(2):
            @pl.when(x != 0)
            def _():
                a_copy(h, 0, l).wait_send()
            for dz in range(1, NZ):
                a_copy(h, dz, l).wait_send()
    for slot in range(1, NX):
        p_copy(slot).wait_send()
        over_x(slot).wait_send()
    for k in range(len(chunks)):
        for cp in y_copies(k)[2] + c_copies(k):
            cp.wait_send()
    for slot in range(NX):
        for h in range(2):
            over_y(slot, h).wait_send()
        for d in range(1, NZ):
            over_z(slot, d).wait_send()


def exchange(idx_a, idx_p, weights, adjoint, primal):
    bf, f32 = jnp.bfloat16, jnp.float32
    dma = pltpu.SemaphoreType.DMA
    smem = pl.BlockSpec(memory_space=pltpu.SMEM)
    hbm = pl.BlockSpec(memory_space=pl.ANY)
    vmem = pl.BlockSpec(memory_space=pltpu.VMEM)
    return pl.pallas_call(
        main_kernel,
        in_specs=[smem, smem, vmem, hbm, hbm],
        out_specs=vmem,
        out_shape=jax.ShapeDtypeStruct((64, 128), f32),
        scratch_shapes=[
            pltpu.VMEM(adjoint.shape, bf),
            pltpu.VMEM(primal.shape, bf),
            pltpu.VMEM((DEV_PEN, 64, PEN), bf),
            pltpu.VMEM((DEV_PEN, 128, PEN), bf),
            pltpu.VMEM((NZ, 2, 2, 32, BLK), bf),
            pltpu.VMEM((NX, 128, KLOC), bf),
            pltpu.VMEM((2, NX, 2, 2, 32, BLK), bf),
            pltpu.VMEM((2, 16, 32, KLOC), bf),
            pltpu.VMEM((NX, 128, KLOC), bf),
            pltpu.VMEM((NX, 2, ROWS, 128), f32),
            pltpu.VMEM((NX, 2, ROWS, 128), bf),
            pltpu.VMEM((NX, 2, ROWS, 128), bf),
            pltpu.VMEM((NX, NZ, 2, 32, 128), f32),
            pltpu.VMEM((NX, NZ, 2, 32, 128), bf),
            pltpu.VMEM((NX, NZ, 2, 32, 128), bf),
            pltpu.VMEM((3, 2, 32, 128), f32),
            pltpu.VMEM((3, 2, 32, 128), f32),
            dma((2,)),
            dma((NZ, 2, 2)), dma((2, NX, 2, 2)),
            dma((3,)), dma((NX,)),
            dma((32, 2)), dma((2, 2, NX, 2, 2)),
            dma((32, 2)), dma((2, 2, NX, 2, 2)),
            dma((NX, 2)), dma((NX, 2)),
            dma((NX, NZ - 1)), dma((NX, NZ)),
            dma((3,)), dma((3,)),
        ],
        compiler_params=pltpu.CompilerParams(
            collective_id=0, has_side_effects=True, vmem_limit_bytes=60 * 1024 * 1024),
        name="exchange",
    )(idx_a.T, idx_p.T, weights[None], adjoint, primal)


def on_device(primal, adjoint_pencils, weights, pencil_map):
    space = lax.axis_index("space")
    maps = pencil_map.reshape(TILES, DEV_PEN)
    target = maps // DEV_PEN
    before = jnp.arange(DEV_PEN)[None, :] < jnp.arange(DEV_PEN)[:, None]
    rank = jnp.sum((target[:, :, None] == target[:, None, :]) & before[None], axis=2, dtype=jnp.int32)
    of_rank = jnp.arange(SHARE, dtype=jnp.int32)[None, :, None]
    here = (target == space)[:, None, :] & (rank[:, None, :] == of_rank)
    idx_p = jnp.sum(jnp.where(here, maps[:, None, :] - space * DEV_PEN, 0), axis=2, dtype=jnp.int32)
    own_target = lax.dynamic_index_in_dim(target, space, 0, keepdims=True)
    own_rank = lax.dynamic_index_in_dim(rank, space, 0, keepdims=True)
    to = (own_target == jnp.arange(TILES, dtype=jnp.int32)[:, None])[:, None, :] & (own_rank[:, None, :] == of_rank)
    idx_a = jnp.sum(jnp.where(to, jnp.arange(DEV_PEN, dtype=jnp.int32), 0), axis=2, dtype=jnp.int32)
    return exchange(idx_a, idx_p, weights, adjoint_pencils, primal)


def solution(mesh):
    placed = (P("snap", "space"), P("snap", "space"), P("space"), P())
    return jax.shard_map(
        on_device, mesh=mesh, in_specs=placed, out_specs=P("space", "snap"), check_vma=False
    )
```

```python
import functools
import jax
import jax.numpy as jnp
from jax import lax
from jax.experimental import pallas as pl
from jax.experimental.pallas import tpu as pltpu
from jax.sharding import PartitionSpec as P

PEN = 128
NX, NZ = 4, 8
TILES = 16
DEV_PEN = 96
SHARE = 6
MESH = pl.DeviceIdType.MESH
BLK = SHARE * PEN
KLOC = 4 * BLK


def where_am_i():
    space = lax.axis_index("space")
    snap = lax.axis_index("snap")
    return space // 2, space % 2, snap // 8, (snap // 2) % NX, snap % 2


def device(z, ylo, yh, x, c):
    return {"space": z * 2 + ylo, "snap": yh * 8 + x * 2 + c}


ORDER = (0, 1, 7, 2, 6, 4, 3, 5)
XORDER = (1, 3, 2)
ROWS = 256


def main_kernel(idx_a, idx_p, w_ref, a_hbm, p_hbm, o_ref, a_v, p_v, a3, p3, asort, psort, r1, afin, pfin,
                keep, ysend, yrecv, zsum, zsend, zrecv, xsend, xrecv,
                lsem, ss1, rs1, ssp, rsp, ssy, rsy, ssc, rsc, ssf, rsf, ssz, rsz, ssx, rsx):
    z, ylo, yh, x, c = where_am_i()

    def remote(src, dst, ss, rs, dev):
        return pltpu.make_async_remote_copy(src_ref=src, dst_ref=dst, send_sem=ss, recv_sem=rs,
                                            device_id=dev, device_id_type=MESH)

    def arrived(ref, sem):
        pltpu.make_async_copy(ref, ref, sem).wait()

    load_a = pltpu.make_async_copy(a_hbm, a_v, lsem.at[0])
    load_p = pltpu.make_async_copy(p_hbm, p_v, lsem.at[1])
    load_a.start()
    load_p.start()

    bar = pltpu.get_barrier_semaphore()

    def greet(dev):
        pl.semaphore_signal(bar, inc=1, device_id=dev, device_id_type=MESH)

    for zi in range(2):
        for xs in range(NX):
            dev = device((z - x - 4 * zi + 2 * NZ) % NZ, ylo, yh, xs, c)
            if zi == 0 and xs == 0:
                @pl.when(x != 0)
                def _():
                    greet(dev)
            else:
                greet(dev)
    for d in range(1, NX):
        greet(device(z, ylo, yh, (x + d) % NX, c))
    greet(device(z, ylo, 1 - yh, x, c))
    greet(device(z, 1 - ylo, 0, x, c))
    greet(device(z, 1 - ylo, 1, x, c))
    greet(device(z, ylo, yh, x, 1 - c))
    for d in range(1, NZ):
        greet(device((z + d) % NZ, ylo, yh, x, c))

    load_a.wait()
    for i in range(DEV_PEN):
        a3[i] = a_v[:, i * PEN:(i + 1) * PEN]
    for dz in range(NZ):
        for lt in range(2):
            t = ((z + dz) % NZ) * 2 + lt
            for r in range(SHARE):
                v = a3[idx_a[r, t]]
                for h in range(2):
                    asort[dz, lt, h, :, r * PEN:(r + 1) * PEN] = v[h * 32:(h + 1) * 32]

    load_p.wait()
    for i in range(DEV_PEN):
        span = slice(i * PEN, (i + 1) * PEN)
        p3[i] = (p_v[:, span].astype(jnp.float32) * w_ref[:, span]).astype(jnp.bfloat16)

    pl.semaphore_wait(bar, 7 + 3 + 3 + 1 + 7 + (x + NX - 1) // NX)

    def a_copy(h, dz, l):
        lt = (1 - ylo + l) % 2
        return remote(asort.at[dz, lt, h], r1.at[dz // NX, x, lt, h], ss1.at[dz, l, h],
                      rs1.at[dz // NX, x, lt, h], device((z + dz) % NZ, ylo, yh, dz % NX, c))

    for h in range(2):
        for dz in ORDER:
            for l in range(2):
                if dz == 0:
                    lt = (1 - ylo + l) % 2

                    @pl.when(x == 0)
                    def _():
                        pltpu.make_async_copy(asort.at[0, lt, h], r1.at[0, 0, lt, h], rs1.at[0, 0, lt, h]).start()

                    @pl.when(x != 0)
                    def _():
                        a_copy(h, 0, l).start()
                else:
                    a_copy(h, dz, l).start()

    def p_copy(slot):
        d = XORDER[slot - 1]
        return remote(psort.at[d], pfin.at[XORDER.index(NX - d) + 1], ssp.at[slot - 1],
                      rsp.at[XORDER.index(NX - d) + 1], device(z, ylo, yh, (x + d) % NX, c))

    own_p = pltpu.make_async_copy(psort.at[0], pfin.at[0], rsp.at[0])
    for step, d in enumerate(XORDER + (0,)):
        for zi in range(2):
            dz = (x + d) % NX + NX * zi
            for ls in range(2):
                src = ((z - dz + NZ) % NZ) * 2 + ls
                for r in range(SHARE):
                    i = idx_p[r, src]
                    at = ((zi * 2 + ls) * SHARE + r) * PEN
                    psort[d, :, at:at + PEN] = p3[i]
        if step >= 1:
            p_copy(step).start()
    own_p.start()

    flip = x // 3
    chunks = [(h, j, d, l) for h in range(2) for j in range(2) for d in (0, 1, 3, 2) for l in range(2)]

    def block(h, ys, xs, core, zi, ls):
        lane = pl.ds(pl.multiple_of((zi * 2 + ls) * BLK, BLK), BLK)
        return afin.at[h, core * NZ + ys * NX + xs, :, lane]

    def y_copies(k):
        h, j, d, l = chunks[k]
        zi, xs, lt = (j + flip) % 2, (x + d) % NX, (1 - ylo + l) % 2
        src = r1.at[zi, xs, lt, h]
        dst = block(h, yh, xs, c, zi, ylo)
        rs = rsy.at[h, yh, xs, zi, ylo]
        out = [remote(src, dst, ssy.at[k, 0], rs, device(z, lt, 1 - yh, x, c))]
        if l == 0:
            out.append(remote(src, dst, ssy.at[k, 1], rs, device(z, lt, yh, x, c)))
        return src, rs1.at[zi, xs, lt, h], out, dst, rs

    def sources(k):
        h, j, d, l = chunks[k]
        zi, xs = (j + flip) % 2, (x + d) % NX
        ls = (ylo + 1 - l) % 2
        return [(h, (yh + dy) % 2, xs, zi, ls, dy) for dy in range(2)]

    def c_copies(k):
        return [remote(block(h, ys, xs, c, zi, ls), block(h, ys, xs, c, zi, ls), ssc.at[k, dy],
                       rsc.at[h, ys, xs, zi, ls], device(z, ylo, yh, x, 1 - c))
                for h, ys, xs, zi, ls, dy in sources(k)]

    lag = 6
    for k in range(len(chunks) + lag):
        if k < len(chunks):
            src, sem, out, dst, rs = y_copies(k)
            arrived(src, sem)
            for cp in out:
                cp.start()
            if chunks[k][3] == 1:
                pltpu.make_async_copy(src, dst, rs).start()
        if k >= lag:
            for (h, ys, xs, zi, ls, _), cp in zip(sources(k - lag), c_copies(k - lag)):
                arrived(block(h, ys, xs, c, zi, ls), rsy.at[h, ys, xs, zi, ls])
                cp.start()
    for k in range(len(chunks)):
        for h, ys, xs, zi, ls, _ in sources(k):
            arrived(block(h, ys, xs, 1 - c, zi, ls), rsc.at[h, ys, xs, zi, ls])

    def lhs(h, l):
        at = pl.multiple_of((ylo + 1 - l) % 2 * NZ, NZ)
        return afin[h, pl.ds(at, NZ)].reshape(ROWS, KLOC)

    def times(a, b):
        return lax.dot_general(a, b, (((1,), (1,)), ((), ())), preferred_element_type=jnp.float32)

    def over_y(slot, h):
        return remote(ysend.at[slot, h], yrecv.at[slot, h], ssf.at[slot, h], rsf.at[slot, h],
                      device(z, 1 - ylo, yh, x, c))

    def over_z(slot, d):
        to = (z + d) % NZ
        return remote(zsend.at[slot, to], zrecv.at[slot, z], ssz.at[slot, d - 1], rsz.at[slot, z],
                      device(to, ylo, yh, x, c))

    def over_x(slot):
        d = XORDER[slot - 1]
        back = XORDER.index(NX - d)
        return remote(xsend.at[slot - 1], xrecv.at[back], ssx.at[slot - 1], rsx.at[back],
                      device(z, ylo, yh, (x + d) % NX, c))

    def to_z(slot):
        for h in range(2):
            arrived(yrecv.at[slot, h], rsf.at[slot, h])
            v = (keep[slot, h] + yrecv[slot, h].astype(jnp.float32)).reshape(NZ, 32, 128)
            zsum[slot, :, h] = v
            zsend[slot, :, h] = v.astype(zsend.dtype)
        for d in (4, 3, 5, 2, 6, 1, 7):
            over_z(slot, d).start()

    def summed(slot):
        acc = zsum[slot, z]
        for d in (1, 7, 2, 6, 3, 5, 4):
            frm = (z + d) % NZ
            arrived(zrecv.at[slot, frm], rsz.at[slot, frm])
            acc = acc + zrecv[slot, frm].astype(jnp.float32)
        return acc

    def pair(base, l):
        for h in range(2):
            v = times(lhs(h, l), pfin[base:base + 2].reshape(256, KLOC))
            for slot in (base, base + 1):
                w = v[:, (slot - base) * 128:(slot - base + 1) * 128]
                if l == 0:
                    ysend[slot, h] = w.astype(ysend.dtype)
                    over_y(slot, h).start()
                else:
                    keep[slot, h] = w

    for base in (0, 2):
        arrived(pfin.at[base], rsp.at[base])
        arrived(pfin.at[base + 1], rsp.at[base + 1])
        pair(base, 0)
    pair(0, 1)
    to_z(1)
    to_z(0)
    pair(2, 1)
    to_z(3)
    to_z(2)
    for slot in (1, 2):
        xsend[slot - 1] = summed(slot)
        over_x(slot).start()
    acc = summed(0)
    xsend[2] = summed(3)
    over_x(3).start()
    for slot in range(3):
        arrived(xrecv.at[slot], rsx.at[slot])
        acc = acc + xrecv[slot]
    o_ref[...] = acc.reshape(64, 128)

    for h in range(2):
        for l in range(2):
            @pl.when(x != 0)
            def _():
                a_copy(h, 0, l).wait_send()
            for dz in range(1, NZ):
                a_copy(h, dz, l).wait_send()
    for slot in range(1, NX):
        p_copy(slot).wait_send()
        over_x(slot).wait_send()
    for k in range(len(chunks)):
        for cp in y_copies(k)[2] + c_copies(k):
            cp.wait_send()
    for slot in range(NX):
        for h in range(2):
            over_y(slot, h).wait_send()
        for d in range(1, NZ):
            over_z(slot, d).wait_send()


def exchange(idx_a, idx_p, weights, adjoint, primal):
    bf, f32 = jnp.bfloat16, jnp.float32
    dma = pltpu.SemaphoreType.DMA
    smem = pl.BlockSpec(memory_space=pltpu.SMEM)
    hbm = pl.BlockSpec(memory_space=pl.ANY)
    vmem = pl.BlockSpec(memory_space=pltpu.VMEM)
    return pl.pallas_call(
        main_kernel,
        in_specs=[smem, smem, vmem, hbm, hbm],
        out_specs=vmem,
        out_shape=jax.ShapeDtypeStruct((64, 128), f32),
        scratch_shapes=[
            pltpu.VMEM(adjoint.shape, bf),
            pltpu.VMEM(primal.shape, bf),
            pltpu.VMEM((DEV_PEN, 64, PEN), bf),
            pltpu.VMEM((DEV_PEN, 128, PEN), bf),
            pltpu.VMEM((NZ, 2, 2, 32, BLK), bf),
            pltpu.VMEM((NX, 128, KLOC), bf),
            pltpu.VMEM((2, NX, 2, 2, 32, BLK), bf),
            pltpu.VMEM((2, 16, 32, KLOC), bf),
            pltpu.VMEM((NX, 128, KLOC), bf),
            pltpu.VMEM((NX, 2, ROWS, 128), f32),
            pltpu.VMEM((NX, 2, ROWS, 128), bf),
            pltpu.VMEM((NX, 2, ROWS, 128), bf),
            pltpu.VMEM((NX, NZ, 2, 32, 128), f32),
            pltpu.VMEM((NX, NZ, 2, 32, 128), bf),
            pltpu.VMEM((NX, NZ, 2, 32, 128), bf),
            pltpu.VMEM((3, 2, 32, 128), f32),
            pltpu.VMEM((3, 2, 32, 128), f32),
            dma((2,)),
            dma((NZ, 2, 2)), dma((2, NX, 2, 2)),
            dma((3,)), dma((NX,)),
            dma((32, 2)), dma((2, 2, NX, 2, 2)),
            dma((32, 2)), dma((2, 2, NX, 2, 2)),
            dma((NX, 2)), dma((NX, 2)),
            dma((NX, NZ - 1)), dma((NX, NZ)),
            dma((3,)), dma((3,)),
        ],
        compiler_params=pltpu.CompilerParams(
            collective_id=0, has_side_effects=True, vmem_limit_bytes=60 * 1024 * 1024),
        name="exchange",
    )(idx_a.T, idx_p.T, weights[None], adjoint, primal)


def on_device(primal, adjoint_pencils, weights, pencil_map):
    space = lax.axis_index("space")
    maps = pencil_map.reshape(TILES, DEV_PEN)
    target = maps // DEV_PEN
    before = jnp.arange(DEV_PEN)[None, :] < jnp.arange(DEV_PEN)[:, None]
    rank = jnp.sum((target[:, :, None] == target[:, None, :]) & before[None], axis=2, dtype=jnp.int32)
    of_rank = jnp.arange(SHARE, dtype=jnp.int32)[None, :, None]
    here = (target == space)[:, None, :] & (rank[:, None, :] == of_rank)
    idx_p = jnp.sum(jnp.where(here, maps[:, None, :] - space * DEV_PEN, 0), axis=2, dtype=jnp.int32)
    own_target = lax.dynamic_index_in_dim(target, space, 0, keepdims=True)
    own_rank = lax.dynamic_index_in_dim(rank, space, 0, keepdims=True)
    to = (own_target == jnp.arange(TILES, dtype=jnp.int32)[:, None])[:, None, :] & (own_rank[:, None, :] == of_rank)
    idx_a = jnp.sum(jnp.where(to, jnp.arange(DEV_PEN, dtype=jnp.int32), 0), axis=2, dtype=jnp.int32)
    return exchange(idx_a, idx_p, weights, adjoint_pencils, primal)


def solution(mesh):
    placed = (P("snap", "space"), P("snap", "space"), P("space"), P())
    return jax.shard_map(
        on_device, mesh=mesh, in_specs=placed, out_specs=P("space", "snap"), check_vma=False
    )
```

```python
import functools
import jax
import jax.numpy as jnp
from jax import lax
from jax.experimental import pallas as pl
from jax.experimental.pallas import tpu as pltpu
from jax.sharding import PartitionSpec as P

PEN = 128
NX, NZ = 4, 8
TILES = 16
DEV_PEN = 96
SHARE = 6
MESH = pl.DeviceIdType.MESH
BLK = SHARE * PEN
KLOC = 4 * BLK


def where_am_i():
    space = lax.axis_index("space")
    snap = lax.axis_index("snap")
    return space // 2, space % 2, snap // 8, (snap // 2) % NX, snap % 2


def device(z, ylo, yh, x, c):
    return {"space": z * 2 + ylo, "snap": yh * 8 + x * 2 + c}


ORDER = (0, 1, 7, 2, 6, 4, 3, 5)
XORDER = (1, 3, 2)
ROWS = 256


def main_kernel(idx_a, idx_p, w_ref, a_hbm, p_hbm, o_ref, a_v, p_v, a3, p3, asort, psort, r1, afin, pfin,
                keep, ysend, yrecv, zsum, zsend, zrecv, xsend, xrecv,
                lsem, ss1, rs1, ssp, rsp, ssy, rsy, ssc, rsc, ssf, rsf, ssz, rsz, ssx, rsx):
    z, ylo, yh, x, c = where_am_i()

    def remote(src, dst, ss, rs, dev):
        return pltpu.make_async_remote_copy(src_ref=src, dst_ref=dst, send_sem=ss, recv_sem=rs,
                                            device_id=dev, device_id_type=MESH)

    def arrived(ref, sem):
        pltpu.make_async_copy(ref, ref, sem).wait()

    load_a = pltpu.make_async_copy(a_hbm, a_v, lsem.at[0])
    load_p = pltpu.make_async_copy(p_hbm, p_v, lsem.at[1])
    load_a.start()
    load_p.start()

    bar = pltpu.get_barrier_semaphore()

    def greet(dev):
        pl.semaphore_signal(bar, inc=1, device_id=dev, device_id_type=MESH)

    for zi in range(2):
        for xs in range(NX):
            dev = device((z - x - 4 * zi + 2 * NZ) % NZ, ylo, yh, xs, c)
            if zi == 0 and xs == 0:
                @pl.when(x != 0)
                def _():
                    greet(dev)
            else:
                greet(dev)
    for d in range(1, NX):
        greet(device(z, ylo, yh, (x + d) % NX, c))
    greet(device(z, ylo, 1 - yh, x, c))
    greet(device(z, 1 - ylo, 0, x, c))
    greet(device(z, 1 - ylo, 1, x, c))
    greet(device(z, ylo, yh, x, 1 - c))
    for d in range(1, NZ):
        greet(device((z + d) % NZ, ylo, yh, x, c))

    load_a.wait()
    for i in range(DEV_PEN):
        a3[i] = a_v[:, i * PEN:(i + 1) * PEN]
    for dz in range(NZ):
        for lt in range(2):
            t = ((z + dz) % NZ) * 2 + lt
            for r in range(SHARE):
                v = a3[idx_a[r, t]]
                for h in range(2):
                    asort[dz, lt, h, :, r * PEN:(r + 1) * PEN] = v[h * 32:(h + 1) * 32]

    load_p.wait()
    for i in range(DEV_PEN):
        span = slice(i * PEN, (i + 1) * PEN)
        p3[i] = (p_v[:, span].astype(jnp.float32) * w_ref[:, span]).astype(jnp.bfloat16)

    def p_copy(slot):
        d = XORDER[slot - 1]
        return remote(psort.at[d], pfin.at[XORDER.index(NX - d) + 1], ssp.at[slot - 1],
                      rsp.at[XORDER.index(NX - d) + 1], device(z, ylo, yh, (x + d) % NX, c))

    own_p = pltpu.make_async_copy(psort.at[0], pfin.at[0], rsp.at[0])
    def sort_p(d):
        for zi in range(2):
            dz = (x + d) % NX + NX * zi
            for ls in range(2):
                src = ((z - dz + NZ) % NZ) * 2 + ls
                for r in range(SHARE):
                    at = ((zi * 2 + ls) * SHARE + r) * PEN
                    psort[d, :, at:at + PEN] = p3[idx_p[r, src]]

    sort_p(1)

    pl.semaphore_wait(bar, 7 + 3 + 3 + 1 + 7 + (x + NX - 1) // NX)

    def a_copy(h, dz, l):
        lt = (1 - ylo + l) % 2
        return remote(asort.at[dz, lt, h], r1.at[dz // NX, x, lt, h], ss1.at[dz, l, h],
                      rs1.at[dz // NX, x, lt, h], device((z + dz) % NZ, ylo, yh, dz % NX, c))

    def send_a(h):
        for dz in ORDER:
            for l in range(2):
                if dz == 0:
                    lt = (1 - ylo + l) % 2

                    @pl.when(x == 0)
                    def _():
                        pltpu.make_async_copy(asort.at[0, lt, h], r1.at[0, 0, lt, h], rs1.at[0, 0, lt, h]).start()

                    @pl.when(x != 0)
                    def _():
                        a_copy(h, 0, l).start()
                else:
                    a_copy(h, dz, l).start()

    p_copy(1).start()
    send_a(0)
    sort_p(3)
    sort_p(2)
    p_copy(2).start()
    sort_p(0)
    p_copy(3).start()
    own_p.start()
    send_a(1)

    flip = x // 3
    chunks = [(h, j, d, l) for h in range(2) for j in range(2) for d in (0, 1, 3, 2) for l in range(2)]

    def block(h, ys, xs, core, zi, ls):
        lane = pl.ds(pl.multiple_of((zi * 2 + ls) * BLK, BLK), BLK)
        return afin.at[h, core * NZ + ys * NX + xs, :, lane]

    def y_copies(k):
        h, j, d, l = chunks[k]
        zi, xs, lt = (j + flip) % 2, (x + d) % NX, (1 - ylo + l) % 2
        src = r1.at[zi, xs, lt, h]
        dst = block(h, yh, xs, c, zi, ylo)
        rs = rsy.at[h, yh, xs, zi, ylo]
        out = [remote(src, dst, ssy.at[k, 0], rs, device(z, lt, 1 - yh, x, c))]
        if l == 0:
            out.append(remote(src, dst, ssy.at[k, 1], rs, device(z, lt, yh, x, c)))
        return src, rs1.at[zi, xs, lt, h], out, dst, rs

    def sources(k):
        h, j, d, l = chunks[k]
        zi, xs = (j + flip) % 2, (x + d) % NX
        ls = (ylo + 1 - l) % 2
        return [(h, (yh + dy) % 2, xs, zi, ls, dy) for dy in range(2)]

    def c_copies(k):
        return [remote(block(h, ys, xs, c, zi, ls), block(h, ys, xs, c, zi, ls), ssc.at[k, dy],
                       rsc.at[h, ys, xs, zi, ls], device(z, ylo, yh, x, 1 - c))
                for h, ys, xs, zi, ls, dy in sources(k)]

    lag = 6
    for k in range(len(chunks) + lag):
        if k < len(chunks):
            src, sem, out, dst, rs = y_copies(k)
            arrived(src, sem)
            for cp in out:
                cp.start()
            if chunks[k][3] == 1:
                pltpu.make_async_copy(src, dst, rs).start()
        if k >= lag:
            for (h, ys, xs, zi, ls, _), cp in zip(sources(k - lag), c_copies(k - lag)):
                arrived(block(h, ys, xs, c, zi, ls), rsy.at[h, ys, xs, zi, ls])
                cp.start()
    for k in range(len(chunks)):
        for h, ys, xs, zi, ls, _ in sources(k):
            arrived(block(h, ys, xs, 1 - c, zi, ls), rsc.at[h, ys, xs, zi, ls])

    def lhs(h, l):
        at = pl.multiple_of((ylo + 1 - l) % 2 * NZ, NZ)
        return afin[h, pl.ds(at, NZ)].reshape(ROWS, KLOC)

    def times(a, b):
        return lax.dot_general(a, b, (((1,), (1,)), ((), ())), preferred_element_type=jnp.float32)

    def over_y(slot, h):
        return remote(ysend.at[slot, h], yrecv.at[slot, h], ssf.at[slot, h], rsf.at[slot, h],
                      device(z, 1 - ylo, yh, x, c))

    def over_z(slot, d):
        to = (z + d) % NZ
        return remote(zsend.at[slot, to], zrecv.at[slot, z], ssz.at[slot, d - 1], rsz.at[slot, z],
                      device(to, ylo, yh, x, c))

    def over_x(slot):
        d = XORDER[slot - 1]
        back = XORDER.index(NX - d)
        return remote(xsend.at[slot - 1], xrecv.at[back], ssx.at[slot - 1], rsx.at[back],
                      device(z, ylo, yh, (x + d) % NX, c))

    def to_z(slot):
        for h in range(2):
            arrived(yrecv.at[slot, h], rsf.at[slot, h])
            v = (keep[slot, h] + yrecv[slot, h].astype(jnp.float32)).reshape(NZ, 32, 128)
            zsum[slot, :, h] = v
            zsend[slot, :, h] = v.astype(zsend.dtype)
        for d in (4, 3, 5, 2, 6, 1, 7):
            over_z(slot, d).start()

    def summed(slot):
        acc = zsum[slot, z]
        for d in (1, 7, 2, 6, 3, 5, 4):
            frm = (z + d) % NZ
            arrived(zrecv.at[slot, frm], rsz.at[slot, frm])
            acc = acc + zrecv[slot, frm].astype(jnp.float32)
        return acc

    def pair(base, l):
        for h in range(2):
            v = times(lhs(h, l), pfin[base:base + 2].reshape(256, KLOC))
            for slot in (base, base + 1):
                w = v[:, (slot - base) * 128:(slot - base + 1) * 128]
                if l == 0:
                    ysend[slot, h] = w.astype(ysend.dtype)
                    over_y(slot, h).start()
                else:
                    keep[slot, h] = w

    for base in (0, 2):
        arrived(pfin.at[base], rsp.at[base])
        arrived(pfin.at[base + 1], rsp.at[base + 1])
        pair(base, 0)
    pair(0, 1)
    to_z(1)
    to_z(0)
    pair(2, 1)
    to_z(3)
    to_z(2)
    for slot in (1, 2):
        xsend[slot - 1] = summed(slot)
        over_x(slot).start()
    acc = summed(0)
    xsend[2] = summed(3)
    over_x(3).start()
    for slot in range(3):
        arrived(xrecv.at[slot], rsx.at[slot])
        acc = acc + xrecv[slot]
    o_ref[...] = acc.reshape(64, 128)

    for h in range(2):
        for l in range(2):
            @pl.when(x != 0)
            def _():
                a_copy(h, 0, l).wait_send()
            for dz in range(1, NZ):
                a_copy(h, dz, l).wait_send()
    for slot in range(1, NX):
        p_copy(slot).wait_send()
        over_x(slot).wait_send()
    for k in range(len(chunks)):
        for cp in y_copies(k)[2] + c_copies(k):
            cp.wait_send()
    for slot in range(NX):
        for h in range(2):
            over_y(slot, h).wait_send()
        for d in range(1, NZ):
            over_z(slot, d).wait_send()


def exchange(idx_a, idx_p, weights, adjoint, primal):
    bf, f32 = jnp.bfloat16, jnp.float32
    dma = pltpu.SemaphoreType.DMA
    smem = pl.BlockSpec(memory_space=pltpu.SMEM)
    hbm = pl.BlockSpec(memory_space=pl.ANY)
    vmem = pl.BlockSpec(memory_space=pltpu.VMEM)
    return pl.pallas_call(
        main_kernel,
        in_specs=[smem, smem, vmem, hbm, hbm],
        out_specs=vmem,
        out_shape=jax.ShapeDtypeStruct((64, 128), f32),
        scratch_shapes=[
            pltpu.VMEM(adjoint.shape, bf),
            pltpu.VMEM(primal.shape, bf),
            pltpu.VMEM((DEV_PEN, 64, PEN), bf),
            pltpu.VMEM((DEV_PEN, 128, PEN), bf),
            pltpu.VMEM((NZ, 2, 2, 32, BLK), bf),
            pltpu.VMEM((NX, 128, KLOC), bf),
            pltpu.VMEM((2, NX, 2, 2, 32, BLK), bf),
            pltpu.VMEM((2, 16, 32, KLOC), bf),
            pltpu.VMEM((NX, 128, KLOC), bf),
            pltpu.VMEM((NX, 2, ROWS, 128), f32),
            pltpu.VMEM((NX, 2, ROWS, 128), bf),
            pltpu.VMEM((NX, 2, ROWS, 128), bf),
            pltpu.VMEM((NX, NZ, 2, 32, 128), f32),
            pltpu.VMEM((NX, NZ, 2, 32, 128), bf),
            pltpu.VMEM((NX, NZ, 2, 32, 128), bf),
            pltpu.VMEM((3, 2, 32, 128), f32),
            pltpu.VMEM((3, 2, 32, 128), f32),
            dma((2,)),
            dma((NZ, 2, 2)), dma((2, NX, 2, 2)),
            dma((3,)), dma((NX,)),
            dma((32, 2)), dma((2, 2, NX, 2, 2)),
            dma((32, 2)), dma((2, 2, NX, 2, 2)),
            dma((NX, 2)), dma((NX, 2)),
            dma((NX, NZ - 1)), dma((NX, NZ)),
            dma((3,)), dma((3,)),
        ],
        compiler_params=pltpu.CompilerParams(
            collective_id=0, has_side_effects=True, vmem_limit_bytes=60 * 1024 * 1024),
        name="exchange",
    )(idx_a.T, idx_p.T, weights[None], adjoint, primal)


def on_device(primal, adjoint_pencils, weights, pencil_map):
    space = lax.axis_index("space")
    maps = pencil_map.reshape(TILES, DEV_PEN)
    target = maps // DEV_PEN
    before = jnp.arange(DEV_PEN)[None, :] < jnp.arange(DEV_PEN)[:, None]
    rank = jnp.sum((target[:, :, None] == target[:, None, :]) & before[None], axis=2, dtype=jnp.int32)
    of_rank = jnp.arange(SHARE, dtype=jnp.int32)[None, :, None]
    here = (target == space)[:, None, :] & (rank[:, None, :] == of_rank)
    idx_p = jnp.sum(jnp.where(here, maps[:, None, :] - space * DEV_PEN, 0), axis=2, dtype=jnp.int32)
    own_target = lax.dynamic_index_in_dim(target, space, 0, keepdims=True)
    own_rank = lax.dynamic_index_in_dim(rank, space, 0, keepdims=True)
    to = (own_target == jnp.arange(TILES, dtype=jnp.int32)[:, None])[:, None, :] & (own_rank[:, None, :] == of_rank)
    idx_a = jnp.sum(jnp.where(to, jnp.arange(DEV_PEN, dtype=jnp.int32), 0), axis=2, dtype=jnp.int32)
    return exchange(idx_a, idx_p, weights, adjoint_pencils, primal)


def solution(mesh):
    placed = (P("snap", "space"), P("snap", "space"), P("space"), P())
    return jax.shard_map(
        on_device, mesh=mesh, in_specs=placed, out_specs=P("space", "snap"), check_vma=False
    )
```
